256 devices in a mesh: expert: 8 (over y, core), shard: 32 (over z, x).
Axes of the slice: x: 4, y: 4, z: 8, core: 2. Of those that a mesh axis runs over, the one named last changes fastest.
Arguments:
- activations: bfloat16 [8, 32, 96, 2048], P('expert', 'shard'), may hold values from -6 to 6
- out_grads: bfloat16 [8, 32, 96, 7168], P('expert', 'shard'), may hold values from -6 to 6
- next_inputs: bfloat16 [8, 32, 96, 2048], P('expert', 'shard'), may hold values from -6 to 6
- counts: int32 [8, 32], P('expert', 'shard'), may hold values from 1 to 96, as said below
- master: float32 [8, 32, 512, 896], P('expert', 'shard'), may hold values from -0.125 to 0.125
- moment: bfloat16 [8, 32, 512, 896], P('expert', 'shard'), may hold values from -6 to 6
- second: bfloat16 [8, 32, 512, 896], P('expert', 'shard'), may hold values from 0.099609375 to 4
Outputs:
- master_new: float32 [8, 32, 512, 896], P('expert', 'shard')
- moment_new: bfloat16 [8, 32, 512, 896], P('expert', 'shard')
- second_new: bfloat16 [8, 32, 512, 896], P('expert', 'shard')
- projected: bfloat16 [8, 32, 96, 7168], P('expert', 'shard')
The draws below stay inside these ranges and needn't reach their ends.
Inputs may be any that keep to these rules, and one draw needn't show every extreme that they name: counts[e, s] of the 96 slots of expert e from shard s hold tokens, the leading ones; the rest are padding.
All inputs are finite; a program needn't handle non-finite values.
Results may differ from the reference program's by a relative error of at most 0.00055.
The reference program's roundings to bfloat16 on the way count: a program that leaves them out, or rounds other values in their place, can miss the bound.
Values may be sent and summed in bfloat16 or wider, within the bound.
No kernel may reach another device: no remote copies, remote signals or barrier semaphores. Data moves between devices by JAX's collectives and lax.ppermute only.
A program may use at most 192 MiB of HBM per device.

```python
import math
import jax
import jax.numpy as jnp
from jax import lax

D = 2048
FF = 7168
CAP = 96
EXPERTS = 8
GRID_R = 4
GRID_C = 8
D_BLK = 512
F_BLK = 896
N_SHARD = 32


def draw_counts(key, part):
    base_key = jax.random.fold_in(key, 7)
    first_key, second_key, third_key, fourth_key = jax.random.split(base_key, 4)
    base = jax.random.randint(first_key, (EXPERTS, N_SHARD), 0, CAP)
    loads = jax.random.randint(second_key, (EXPERTS, 1), 2, 5)
    result = 1 + base * loads // 4
    expert_pick = jax.random.randint(third_key, (), 0, EXPERTS)
    shard_pick = jax.random.randint(fourth_key, (), 0, N_SHARD)
    result = result.at[expert_pick, shard_pick].set(CAP)
    return result.astype(jnp.int32)


def block_scale(rng, dims, cuts, low, high):
    loudness = 1.0
    for axis_at, parts in cuts:
        draws = jax.random.uniform(jax.random.fold_in(jax.random.fold_in(rng, 6), axis_at), (parts,), jnp.float32, low / len(cuts), high / len(cuts))
        loudness = loudness * jnp.repeat(jnp.exp(draws), dims[axis_at] // parts).reshape((-1,) + (1,) * (len(dims) - 1 - axis_at))
    return loudness


def scatter_about(key, dims, width, limit, cuts=(), held_as=jnp.bfloat16):
    values = width * jax.random.normal(key, dims, jnp.float32)
    if cuts:
        values = values * block_scale(key, dims, cuts, -0.22, 0.18)
    return jnp.clip(values, -limit, limit).astype(held_as)


def setup_inputs(seed: int = 0) -> dict:
    key_of = jax.random.split(jax.random.key(seed), 8)
    return {
        "activations": scatter_about(key_of[0], (EXPERTS, N_SHARD, CAP, D), 1.0, 6.0, ((0, 8), (1, 32))),
        "out_grads": scatter_about(key_of[1], (EXPERTS, N_SHARD, CAP, FF), 1.0, 6.0, ((0, 8), (1, 32))),
        "next_inputs": scatter_about(key_of[2], (EXPERTS, N_SHARD, CAP, D), 1.0, 6.0, ((0, 8), (1, 32))),
        "counts": draw_counts(jax.random.fold_in(key_of[7], 71), 0),
        "master": scatter_about(key_of[4], (EXPERTS, N_SHARD, D_BLK, F_BLK), D ** -0.5, 0.125, ((0, 8), (1, 32)), jnp.float32),
        "moment": scatter_about(key_of[5], (EXPERTS, N_SHARD, D_BLK, F_BLK), 1.0, 6.0, ((0, 8), (1, 32))),
        "second": jnp.clip(jnp.exp(math.log(4.0) - 3.6927934 * jax.random.uniform(key_of[6], (EXPERTS, N_SHARD, D_BLK, F_BLK), jnp.float32) ** block_scale(key_of[6], (EXPERTS, N_SHARD, D_BLK, F_BLK), ((0, 8), (1, 32)), -0.2, 0.2)), 0.099609375, 4.0).astype(jnp.bfloat16),
    }


def to_full(tiles):
    return tiles.reshape(EXPERTS, GRID_R, GRID_C, D_BLK, F_BLK).transpose(0, 1, 3, 2, 4).reshape(EXPERTS, D, FF)

def to_tiles(full):
    return full.reshape(EXPERTS, GRID_R, D_BLK, GRID_C, F_BLK).transpose(0, 1, 3, 2, 4).reshape(EXPERTS, N_SHARD, D_BLK, F_BLK)

def expert_grad(couple):
    inputs_here, grads_here = couple
    return jnp.dot(inputs_here.reshape(-1, D).T, grads_here.reshape(-1, FF), preferred_element_type=jnp.float32)

def expert_project(couple):
    inputs_here, matrix = couple
    return jnp.dot(inputs_here.reshape(-1, D), matrix, preferred_element_type=jnp.float32).astype(jnp.bfloat16)

def reference(activations, out_grads, next_inputs, counts, master, moment, second):
    slots = jnp.arange(CAP, dtype=jnp.int32)
    valid = slots[None, None, :] < counts[:, :, None]
    masked = jnp.where(valid[..., None], out_grads, jnp.zeros((), jnp.bfloat16))
    gradient = lax.map(expert_grad, (activations, masked))
    weights = to_full(master)
    first = to_full(moment).astype(jnp.float32)
    later = to_full(second).astype(jnp.float32)
    entries = float(EXPERTS * D * FF)
    grad_rms = jnp.sqrt(jnp.sum(gradient * gradient) / entries + 1e-06)
    clip_factor = jnp.minimum(1.0, 1.0 / grad_rms)
    clipped = clip_factor * gradient
    first_new = 0.9 * first + 0.1 * clipped
    later_new = 0.999 * later + 0.001 * clipped * clipped
    update = first_new / (1.0 - 0.9 ** 10) / (jnp.sqrt(later_new / (1.0 - 0.999 ** 10)) + 1e-06) + 0.01 * weights
    weight_sq = lax.optimization_barrier(jnp.sum(weights * weights, axis=(1, 2)))
    update_sq = lax.optimization_barrier(jnp.sum(update * update, axis=(1, 2)))
    trust_ratio = jnp.sqrt(weight_sq) / (jnp.sqrt(update_sq) + 1e-06)
    weights_new = weights - 0.08 * trust_ratio[:, None, None] * update
    rounded = weights_new.astype(jnp.bfloat16)
    projected = lax.map(expert_project, (next_inputs, rounded)).reshape(EXPERTS, N_SHARD, CAP, FF)
    return (to_tiles(weights_new), to_tiles(first_new).astype(jnp.bfloat16), to_tiles(later_new).astype(jnp.bfloat16), projected)
```

```python
import functools

import jax
import jax.numpy as jnp
from jax import lax
from jax.experimental import pallas as pl
from jax.experimental.pallas import tpu as pltpu
from jax.sharding import Mesh
from jax.sharding import PartitionSpec as P

GRID_R = 4
GRID_C = 8
EXPERT = ("y", "k")
SHARD = ("z", "x")
EVERYONE = ("y", "k", "z", "x")


def totals(values, axes):
    size = lax.axis_size(axes)
    mine = jnp.stack(values)
    sent = jnp.broadcast_to(mine[None, None], (size, 1, len(values)))
    got = lax.all_to_all(sent, axes, 0, 0, tiled=True)
    return jnp.sum(got, axis=(0, 1))


def project(tokens, tiles):
    count, _ = tokens.shape
    grid_r, parities, d_blk, f_blk = tiles.shape

    def kernel(x_ref, w_ref, o_ref, acc_ref):
        step = pl.program_id(1)
        partial = jnp.dot(x_ref[...], w_ref[0, 0], preferred_element_type=jnp.float32)

        @pl.when(step == 0)
        def _():
            acc_ref[...] = partial

        @pl.when(step > 0)
        def _():
            acc_ref[...] += partial

        @pl.when(step == grid_r - 1)
        def _():
            o_ref[0] = acc_ref[...].astype(o_ref.dtype)

    return pl.pallas_call(
        kernel,
        grid=(parities, grid_r),
        in_specs=[
            pl.BlockSpec((count, d_blk), lambda p, r: (0, r)),
            pl.BlockSpec((1, 1, d_blk, f_blk), lambda p, r: (r, p, 0, 0)),
        ],
        out_specs=pl.BlockSpec((1, count, f_blk), lambda p, r: (p, 0, 0)),
        out_shape=jax.ShapeDtypeStruct((parities, count, f_blk), jnp.bfloat16),
        scratch_shapes=[pltpu.VMEM((count, f_blk), jnp.float32)],
        name="project",
    )(tokens, tiles)


def body(activations, out_grads, next_inputs, counts, master, moment, second):
    cap, d = activations.shape[2:]
    ff = out_grads.shape[3]
    d_blk, f_blk = master.shape[2:]
    size_z, size_x = lax.axis_size("z"), lax.axis_size("x")
    parities = GRID_C // size_x
    parity = lax.axis_index("z") % parities

    valid = lax.iota(jnp.int32, cap) < counts[0, 0]
    masked = jnp.where(valid[:, None], out_grads[0, 0], jnp.zeros((), jnp.bfloat16))
    cols = masked.reshape(cap, parities, size_x, f_blk).transpose(2, 1, 0, 3)
    cols = lax.all_to_all(cols, "x", 0, 0, tiled=True)
    cols = lax.all_gather(cols.transpose(1, 0, 2, 3), "z")
    cols = lax.dynamic_index_in_dim(cols, parity, 1, keepdims=False)

    rows = activations[0, 0].reshape(cap, GRID_R, d_blk).transpose(1, 0, 2)
    rows = jnp.repeat(rows, size_z // GRID_R, axis=0)
    rows = lax.all_to_all(rows, "z", 0, 0, tiled=True)
    rows = lax.all_gather(rows, "x")

    gradient = jnp.einsum("xzci,zxcj->ij", rows, cols, preferred_element_type=jnp.float32)

    tokens = lax.all_gather(next_inputs[0, 0], "x").reshape(size_x * cap, d)

    weights = master[0, 0]
    first = moment[0, 0].astype(jnp.float32)
    later = second[0, 0].astype(jnp.float32)
    entries = float(lax.axis_size(EXPERT) * d * ff)
    (norm_total,) = totals([jnp.sum(gradient * gradient)], EVERYONE)
    grad_rms = jnp.sqrt(norm_total / entries + 1e-06)
    clip_factor = jnp.minimum(1.0, 1.0 / grad_rms)
    clipped = clip_factor * gradient
    first_new = 0.9 * first + 0.1 * clipped
    later_new = 0.999 * later + 0.001 * clipped * clipped
    update = (
        first_new / (1.0 - 0.9**10) / (jnp.sqrt(later_new / (1.0 - 0.999**10)) + 1e-06)
        + 0.01 * weights
    )
    weight_sq, update_sq = totals([jnp.sum(weights * weights), jnp.sum(update * update)], SHARD)
    trust_ratio = jnp.sqrt(weight_sq) / (jnp.sqrt(update_sq) + 1e-06)
    weights_new = weights - 0.08 * trust_ratio * update

    tiles = lax.all_gather(weights_new.astype(jnp.bfloat16), "z")
    tiles = tiles.reshape(GRID_R, parities, d_blk, f_blk)
    found = project(tokens, tiles).reshape(parities, size_x, cap, f_blk)
    found = lax.all_to_all(found, "x", 1, 1, tiled=True)
    projected = found.transpose(2, 0, 1, 3).reshape(cap, ff)
    return (
        weights_new[None, None],
        first_new.astype(jnp.bfloat16)[None, None],
        later_new.astype(jnp.bfloat16)[None, None],
        projected[None, None],
    )


def solution(mesh):
    finer = Mesh(mesh.devices.reshape(4, 2, 8, 4), EVERYONE)
    tiled = P(EXPERT, SHARD, None, None)
    return jax.shard_map(
        body,
        mesh=finer,
        in_specs=(tiled, tiled, tiled, P(EXPERT, SHARD), tiled, tiled, tiled),
        out_specs=(tiled,) * 4,
        check_vma=False,
    )
```

```python
import functools

import jax
import jax.numpy as jnp
from jax import lax
from jax.experimental import pallas as pl
from jax.experimental.pallas import tpu as pltpu
from jax.sharding import Mesh
from jax.sharding import PartitionSpec as P

GRID_R = 4
GRID_C = 8
EXPERT = ("y", "k")
SHARD = ("z", "x")
EVERYONE = ("y", "k", "z", "x")


def shift(value, axis, by):
    size = lax.axis_size(axis)
    return lax.ppermute(value, axis, [(i, (i + by) % size) for i in range(size)])


VMEM_LIMIT = 20 << 20
ANYWHERE = pl.BlockSpec(memory_space=pl.ANY)
IN_VMEM = pl.BlockSpec(memory_space=pltpu.VMEM)
IN_SMEM = pl.BlockSpec(memory_space=pltpu.SMEM)


def split(counts, activations, out_grads, d_blk, f_blk):
    cap = activations.shape[0]
    size_x = out_grads.shape[1] // (2 * f_blk)

    def kernel(count_ref, rows_ref, cols_ref, own_ref, other_ref, *row_refs):
        z = lax.axis_index("z")
        q = lax.rem(z, 2)
        valid = lax.broadcasted_iota(jnp.int32, (cap, f_blk), 0) < count_ref[0, 0]
        for i, by in enumerate((0, 1, 3, 2)):
            start = pl.multiple_of(lax.rem(z // 2 + by, GRID_R) * d_blk, 128)
            row_refs[i][...] = rows_ref[:, pl.ds(start, d_blk)]
        for ref, parity in ((own_ref, q), (other_ref, 1 - q)):
            for to_x in range(size_x):
                start = pl.multiple_of((parity * size_x + to_x) * f_blk, 128)
                block = cols_ref[:, pl.ds(start, f_blk)].astype(jnp.float32)
                ref[to_x] = jnp.where(valid, block, 0.0).astype(jnp.bfloat16)

    cols = jax.ShapeDtypeStruct((size_x, cap, f_blk), jnp.bfloat16)
    row = jax.ShapeDtypeStruct((cap, d_blk), jnp.bfloat16)
    return pl.pallas_call(
        kernel,
        in_specs=[IN_SMEM, IN_VMEM, IN_VMEM],
        out_specs=[IN_VMEM] * 6,
        out_shape=[cols] * 2 + [row] * 4,
        compiler_params=pltpu.CompilerParams(vmem_limit_bytes=VMEM_LIMIT),
        name="split",
    )(counts, activations, out_grads)


def fetch(copies, sems):
    started = [pltpu.make_async_copy(src, dst, sems.at[i]) for i, (src, dst) in enumerate(copies)]
    for copy in started:
        copy.start()
    for copy in started:
        copy.wait()


def by_lane(values):
    values = jnp.sum(values, axis=0, keepdims=True)
    return sum(values[:, i : i + 128] for i in range(0, values.shape[1], 128))


def across(values):
    return jnp.sum(jnp.sum(values, axis=0, keepdims=True), axis=1, keepdims=True)


def exchanged(values, axes):
    return lax.all_to_all(values, axes, 0, 0, tiled=True)


def update_of(squares, gradient, master, moment, second, entries):
    d_blk, f_blk = gradient.shape
    steps = 4
    rows = d_blk // steps
    peers = lax.axis_size(SHARD)

    def kernel(n_ref, g_ref, w_ref, m_ref, v_ref, u_ref, m_out, v_out, sums_ref, clip_ref, acc_ref):
        step = pl.program_id(0)

        @pl.when(step == 0)
        def _():
            grad_rms = jnp.sqrt(across(n_ref[:, 0, :]) / entries + 1e-06)
            clip_ref[...] = jnp.broadcast_to(jnp.minimum(1.0, 1.0 / grad_rms), clip_ref.shape)
            acc_ref[...] = jnp.zeros_like(acc_ref)

        weights = w_ref[...]
        clipped = clip_ref[0:1, 0:1] * g_ref[...]
        first_new = 0.9 * m_ref[...].astype(jnp.float32) + 0.1 * clipped
        later_new = 0.999 * v_ref[...].astype(jnp.float32) + 0.001 * clipped * clipped
        update = (
            first_new / (1.0 - 0.9**10) / (jnp.sqrt(later_new / (1.0 - 0.999**10)) + 1e-06)
            + 0.01 * weights
        )
        u_ref[...] = update
        m_out[...] = first_new.astype(jnp.bfloat16)
        v_out[...] = later_new.astype(jnp.bfloat16)
        acc_ref[0:1, :] += by_lane(weights * weights)
        acc_ref[1:2, :] += by_lane(update * update)

        @pl.when(step == steps - 1)
        def _():
            sums_ref[...] = jnp.broadcast_to(acc_ref[0:2, :][None], sums_ref.shape)

    block = pl.BlockSpec((rows, f_blk), lambda i: (i, 0))
    return pl.pallas_call(
        kernel,
        grid=(steps,),
        in_specs=[pl.BlockSpec(squares.shape, lambda i: (0, 0, 0))] + [block] * 4,
        out_specs=[block] * 3 + [pl.BlockSpec((peers, 2, 128), lambda i: (0, 0, 0))],
        out_shape=[
            jax.ShapeDtypeStruct((d_blk, f_blk), jnp.float32),
            jax.ShapeDtypeStruct((d_blk, f_blk), jnp.bfloat16),
            jax.ShapeDtypeStruct((d_blk, f_blk), jnp.bfloat16),
            jax.ShapeDtypeStruct((peers, 2, 128), jnp.float32),
        ],
        scratch_shapes=[pltpu.VMEM((8, 128), jnp.float32), pltpu.VMEM((8, 128), jnp.float32)],
        compiler_params=pltpu.CompilerParams(vmem_limit_bytes=VMEM_LIMIT),
        name="update_of",
    )(squares, gradient, master, moment, second)


def weights_of(sums, update, master):
    d_blk, f_blk = update.shape
    steps = 4
    rows = d_blk // steps

    def kernel(sums_ref, u_ref, w_ref, out_ref, upper_ref, lower_ref, rate_ref):
        step = pl.program_id(0)

        @pl.when(step == 0)
        def _():
            weight_sq = across(sums_ref[:, 0, :])
            update_sq = across(sums_ref[:, 1, :])
            trust_ratio = jnp.sqrt(weight_sq) / (jnp.sqrt(update_sq) + 1e-06)
            rate_ref[...] = jnp.broadcast_to(0.08 * trust_ratio, rate_ref.shape)

        new = w_ref[...] - rate_ref[0:1, 0:1] * u_ref[...]
        out_ref[...] = new

        @pl.when(step < steps // 2)
        def _():
            upper_ref[...] = new.astype(jnp.bfloat16)

        @pl.when(step >= steps // 2)
        def _():
            lower_ref[...] = new.astype(jnp.bfloat16)

    block = pl.BlockSpec((rows, f_blk), lambda i: (i, 0))
    half = jax.ShapeDtypeStruct((d_blk // 2, f_blk), jnp.bfloat16)
    return pl.pallas_call(
        kernel,
        grid=(steps,),
        in_specs=[pl.BlockSpec(sums.shape, lambda i: (0, 0, 0)), block, block],
        out_specs=[
            block,
            pl.BlockSpec((rows, f_blk), lambda i: (jnp.minimum(i, steps // 2 - 1), 0)),
            pl.BlockSpec((rows, f_blk), lambda i: (jnp.maximum(i - steps // 2, 0), 0)),
        ],
        out_shape=[jax.ShapeDtypeStruct((d_blk, f_blk), jnp.float32), half, half],
        scratch_shapes=[pltpu.VMEM((8, 128), jnp.float32)],
        compiler_params=pltpu.CompilerParams(vmem_limit_bytes=VMEM_LIMIT),
        name="weights_of",
    )(sums, update, master)


def outer_sum(rows, places, pieces, before=None, last=False):
    size_x, _, cap, d_blk = rows.shape
    f_blk = pieces[0][0].shape[-1]
    flat = [part for piece in pieces for part in piece]
    depth = size_x * cap
    n = len(pieces)

    def kernel(*refs):
        refs = list(refs)
        rows_ref = refs.pop(0)
        flat_refs = [refs.pop(0) for _ in flat]
        before_ref = refs.pop(0) if before is not None else None
        total_ref = refs.pop(0)
        square_ref = refs.pop(0) if last else None
        left, right, sems = refs
        q = lax.rem(lax.axis_index("z"), 2)
        copies = []
        at = 0
        for i, piece in enumerate(pieces):
            start = 0
            for part in piece:
                size = part.shape[0]
                copies.append((flat_refs[at], right.at[i, pl.ds(start, size)]))
                start += size
                at += 1
            copies.append((rows_ref.at[:, places[i](q)], left.at[i]))
        fetch(copies, sems)
        if before is None:
            total_ref[...] = jnp.zeros_like(total_ref)
        else:
            total_ref[...] = before_ref[...]

        def add(i, carry):
            total_ref[...] += lax.dot_general(
                left[i].reshape(depth, d_blk),
                right[i].reshape(depth, f_blk),
                (((0,), (0,)), ((), ())),
                preferred_element_type=jnp.float32,
            )
            return carry

        lax.fori_loop(0, n, add, 0)
        if last:
            value = total_ref[...]
            square_ref[...] = jnp.broadcast_to(by_lane(value * value)[None], square_ref.shape)

    operands = [rows, *flat]
    in_specs = [ANYWHERE] * len(operands)
    aliases = {}
    if before is not None:
        aliases = {len(operands): 0}
        operands.append(before)
        in_specs.append(IN_VMEM)
    out_shape = [jax.ShapeDtypeStruct((d_blk, f_blk), jnp.float32)]
    if last:
        out_shape.append(jax.ShapeDtypeStruct((lax.axis_size(EVERYONE), 1, 128), jnp.float32))
    return pl.pallas_call(
        kernel,
        in_specs=in_specs,
        out_specs=[IN_VMEM] * len(out_shape),
        out_shape=out_shape,
        scratch_shapes=[
            pltpu.VMEM((n, size_x, cap, d_blk), jnp.bfloat16),
            pltpu.VMEM((n, size_x, cap, f_blk), jnp.bfloat16),
            pltpu.SemaphoreType.DMA((len(flat) + n,)),
        ],
        input_output_aliases=aliases,
        cost_estimate=pl.CostEstimate(
            flops=2 * n * depth * d_blk * f_blk,
            bytes_accessed=n * depth * (d_blk + f_blk) * 2 + 4 * d_blk * f_blk,
            transcendentals=0,
        ),
        compiler_params=pltpu.CompilerParams(vmem_limit_bytes=VMEM_LIMIT),
        name="outer_last" if last else "outer_first",
    )(*operands)


def project(tokens, tiles, before=None):
    size_x, cap, d = tokens.shape
    d_blk = d // GRID_R
    f_blk = tiles[0][1][0].shape[-1]
    flat = [part for _, piece in tiles for part in piece]
    evens = [i for i, (away, _) in enumerate(tiles) if away % 2 == 0]
    odds = [i for i, (away, _) in enumerate(tiles) if away % 2]
    assert evens + odds == list(range(len(tiles)))
    count = size_x * cap
    n = len(tiles)

    def kernel(*refs):
        refs = list(refs)
        tokens_ref = refs.pop(0)
        flat_refs = [refs.pop(0) for _ in flat]
        before_ref = None if before is None else refs.pop(0)
        out_ref, left, right, total, sems = refs
        z = lax.axis_index("z")
        copies = []
        at = 0
        for i, (away, piece) in enumerate(tiles):
            start = 0
            for part in piece:
                size = part.shape[0]
                copies.append((flat_refs[at], right.at[i, pl.ds(start, size)]))
                start += size
                at += 1
            block = lax.rem(z + away + 8, 8) // 2
            columns = pl.ds(pl.multiple_of(block * d_blk, 128), d_blk)
            copies.append((tokens_ref.at[:, :, columns], left.at[i]))
        fetch(copies, sems)

        def add(i, carry):
            total[...] += jnp.dot(
                left[i].reshape(count, d_blk), right[i], preferred_element_type=jnp.float32
            )
            return carry

        for i, steps in enumerate(((0, len(evens)), (len(evens), n))):
            total[...] = jnp.zeros_like(total) if before is None else before_ref[i]
            lax.fori_loop(*steps, add, 0)
            if before is None:
                out_ref[i] = total[...]
            else:
                out_ref[:, i] = total[...].astype(jnp.bfloat16).reshape(size_x, cap, f_blk)

    if before is None:
        out_shape = jax.ShapeDtypeStruct((2, count, f_blk), jnp.float32)
    else:
        out_shape = jax.ShapeDtypeStruct((size_x, 2, cap, f_blk), jnp.bfloat16)
    operands = [tokens, *flat] + ([] if before is None else [before])
    return pl.pallas_call(
        kernel,
        in_specs=[ANYWHERE] * (1 + len(flat)) + [IN_VMEM] * (len(operands) - 1 - len(flat)),
        out_specs=IN_VMEM,
        out_shape=out_shape,
        scratch_shapes=[
            pltpu.VMEM((n, size_x, cap, d_blk), jnp.bfloat16),
            pltpu.VMEM((n, d_blk, f_blk), jnp.bfloat16),
            pltpu.VMEM((count, f_blk), jnp.float32),
            pltpu.SemaphoreType.DMA((len(flat) + n,)),
        ],
        cost_estimate=pl.CostEstimate(
            flops=2 * n * count * d_blk * f_blk,
            bytes_accessed=n * d_blk * (count + f_blk) * 2,
            transcendentals=0,
        ),
        compiler_params=pltpu.CompilerParams(vmem_limit_bytes=VMEM_LIMIT),
        name="project_first" if before is None else "project_last",
    )(*operands)


def assemble(found):
    size_x, _, cap, f_blk = found.shape

    def kernel(found_ref, out_ref):
        q = lax.rem(lax.axis_index("z"), 2)
        for i in range(2):
            parity = q if i == 0 else 1 - q
            for j in range(size_x):
                start = pl.multiple_of((parity * size_x + j) * f_blk, 128)
                out_ref[:, pl.ds(start, f_blk)] = found_ref[j, i]

    return pl.pallas_call(
        kernel,
        in_specs=[IN_VMEM],
        out_specs=IN_VMEM,
        out_shape=jax.ShapeDtypeStruct((cap, 2 * size_x * f_blk), found.dtype),
        compiler_params=pltpu.CompilerParams(vmem_limit_bytes=VMEM_LIMIT),
        name="assemble",
    )(found)


def body(activations, out_grads, next_inputs, counts, master, moment, second):
    cap, d = activations.shape[2:]
    ff = out_grads.shape[3]
    d_blk, f_blk = master.shape[2:]
    size_x = lax.axis_size("x")

    own, other, row0, row_p1, row_m1, row_2 = split(
        counts, activations[0, 0], out_grads[0, 0], d_blk, f_blk
    )

    rows = [row0, shift(row_p1, "z", 2), shift(row_m1, "z", -2), shift(row_2, "z", 4)]
    other = exchanged(other, "x")
    rows = jnp.stack(rows)
    place_of = {
        0: lambda q: 0,
        -2: lambda q: 1,
        2: lambda q: 2,
        4: lambda q: 3,
        1: lambda q: 4 + 2 * q,
        -1: lambda q: 5 - q,
        3: lambda q: 6 + q,
        -3: lambda q: 7 - 2 * q,
    }

    other_m1, other_p1 = shift(other, "z", 1), shift(other, "z", -1)
    own, rows, other_m1, other_p1 = lax.optimization_barrier((own, rows, other_m1, other_p1))
    beside = lax.ppermute(rows, "z", [(i, i ^ 1) for i in range(lax.axis_size("z"))])
    rows = lax.all_gather(jnp.concatenate([rows, beside]), "x")
    own = exchanged(own, "x")
    other_m3, other_p3 = shift(other_m1, "z", 2), shift(other_p1, "z", -2)
    own, other_m3, other_p3 = lax.optimization_barrier((own, other_m3, other_p3))
    own_m2, own_p2 = shift(own, "z", 2), shift(own, "z", -2)
    pieces = {0: [own], -1: [other_m1], 1: [other_p1], -3: [other_m3], 3: [other_p3]}
    pieces |= {-2: [own_m2], 2: [own_p2]}
    first_away = (0, -1, 1, -3, 3)
    last_away = (-2, 2, 4)
    (gradient,) = outer_sum(
        rows, [place_of[a] for a in first_away], [pieces[a] for a in first_away]
    )
    half = size_x // 2
    up, down = own_m2[:half], own_p2[half:]
    pieces[4] = [shift(up, "z", 2), shift(down, "z", -2)]
    late_inputs, gradient = lax.optimization_barrier((next_inputs[0, 0], gradient))
    tokens = lax.all_gather(late_inputs, "x")
    gradient, squares = outer_sum(
        rows,
        [place_of[a] for a in last_away],
        [pieces[a] for a in last_away],
        before=gradient,
        last=True,
    )

    entries = float(lax.axis_size(EXPERT) * d * ff)
    update, first_new, later_new, sums = update_of(
        exchanged(squares, EVERYONE), gradient, master[0, 0], moment[0, 0], second[0, 0], entries
    )
    weights_new, upper, lower = weights_of(exchanged(sums, SHARD), update, master[0, 0])

    up = [[upper], [lower]]
    down = [[upper], [lower]]
    for step in range(1, 4):
        for c in range(2):
            up[c].append(shift(up[c][-1], "z", 1))
            down[c].append(shift(down[c][-1], "z", -1))
    tiles = [(0, [upper, lower])]
    for away in (2, 1):
        tiles.append((-away, [up[0][away], up[1][away]]))
        tiles.append((away, [down[0][away], down[1][away]]))
    part = project(tokens, tiles)
    part, last_up, last_down = lax.optimization_barrier((part, up[0][3], down[1][3]))
    tiles = [(4, [shift(last_up, "z", 1), shift(last_down, "z", -1)])]
    tiles.append((-3, [up[0][3], up[1][3]]))
    tiles.append((3, [down[0][3], down[1][3]]))
    found = project(tokens, tiles, before=part)
    projected = assemble(exchanged(found, "x"))
    return (
        weights_new[None, None],
        first_new[None, None],
        later_new[None, None],
        projected[None, None],
    )


def solution(mesh):
    finer = Mesh(mesh.devices.reshape(4, 2, 8, 4), EVERYONE)
    tiled = P(EXPERT, SHARD, None, None)
    return jax.shard_map(
        body,
        mesh=finer,
        in_specs=(tiled, tiled, tiled, P(EXPERT, SHARD), tiled, tiled, tiled),
        out_specs=(tiled,) * 4,
        check_vma=False,
    )
```

```python
import functools

import jax
import jax.numpy as jnp
from jax import lax
from jax.experimental import pallas as pl
from jax.experimental.pallas import tpu as pltpu
from jax.sharding import Mesh
from jax.sharding import PartitionSpec as P

GRID_R = 4
GRID_C = 8
EXPERT = ("y", "k")
SHARD = ("z", "x")
EVERYONE = ("y", "k", "z", "x")


def shift(value, axis, by):
    size = lax.axis_size(axis)
    return lax.ppermute(value, axis, [(i, (i + by) % size) for i in range(size)])


VMEM_LIMIT = 20 << 20
ANYWHERE = pl.BlockSpec(memory_space=pl.ANY)
IN_VMEM = pl.BlockSpec(memory_space=pltpu.VMEM)
IN_SMEM = pl.BlockSpec(memory_space=pltpu.SMEM)


def split(counts, activations, out_grads, d_blk, f_blk):
    cap = activations.shape[0]
    size_x = out_grads.shape[1] // (2 * f_blk)

    def kernel(count_ref, rows_ref, cols_ref, own_ref, other_ref, *row_refs):
        z = lax.axis_index("z")
        q = lax.rem(z, 2)
        valid = lax.broadcasted_iota(jnp.int32, (cap, f_blk), 0) < count_ref[0, 0]
        for i, by in enumerate((0, 1, 3, 2)):
            start = pl.multiple_of(lax.rem(z // 2 + by, GRID_R) * d_blk, 128)
            row_refs[i][...] = rows_ref[:, pl.ds(start, d_blk)]
        for ref, parity in ((own_ref, q), (other_ref, 1 - q)):
            for to_x in range(size_x):
                start = pl.multiple_of((parity * size_x + to_x) * f_blk, 128)
                block = cols_ref[:, pl.ds(start, f_blk)].astype(jnp.float32)
                ref[to_x] = jnp.where(valid, block, 0.0).astype(jnp.bfloat16)

    cols = jax.ShapeDtypeStruct((size_x, cap, f_blk), jnp.bfloat16)
    row = jax.ShapeDtypeStruct((cap, d_blk), jnp.bfloat16)
    return pl.pallas_call(
        kernel,
        in_specs=[IN_SMEM, IN_VMEM, IN_VMEM],
        out_specs=[IN_VMEM] * 6,
        out_shape=[cols] * 2 + [row] * 4,
        compiler_params=pltpu.CompilerParams(vmem_limit_bytes=VMEM_LIMIT),
        name="split",
    )(counts, activations, out_grads)


def fetch(copies, sems):
    started = [pltpu.make_async_copy(src, dst, sems.at[i]) for i, (src, dst) in enumerate(copies)]
    for copy in started:
        copy.start()
    for copy in started:
        copy.wait()


def by_lane(values):
    values = jnp.sum(values, axis=0, keepdims=True)
    return sum(values[:, i : i + 128] for i in range(0, values.shape[1], 128))


def across(values):
    return jnp.sum(jnp.sum(values, axis=0, keepdims=True), axis=1, keepdims=True)


def exchanged(values, axes):
    return lax.all_to_all(values, axes, 0, 0, tiled=True)


def update_of(squares, gradient, master, moment, second, entries):
    d_blk, f_blk = gradient.shape
    steps = 4
    rows = d_blk // steps
    peers = lax.axis_size(SHARD)

    def kernel(n_ref, g_ref, w_ref, m_ref, v_ref, u_ref, m_out, v_out, sums_ref, clip_ref, acc_ref):
        step = pl.program_id(0)

        @pl.when(step == 0)
        def _():
            grad_rms = jnp.sqrt(across(n_ref[:, 0, :]) / entries + 1e-06)
            clip_ref[...] = jnp.broadcast_to(jnp.minimum(1.0, 1.0 / grad_rms), clip_ref.shape)
            acc_ref[...] = jnp.zeros_like(acc_ref)

        weights = w_ref[...]
        clipped = clip_ref[0:1, 0:1] * g_ref[...]
        first_new = 0.9 * m_ref[...].astype(jnp.float32) + 0.1 * clipped
        later_new = 0.999 * v_ref[...].astype(jnp.float32) + 0.001 * clipped * clipped
        update = (
            first_new / (1.0 - 0.9**10) / (jnp.sqrt(later_new / (1.0 - 0.999**10)) + 1e-06)
            + 0.01 * weights
        )
        u_ref[...] = update
        m_out[...] = first_new.astype(jnp.bfloat16)
        v_out[...] = later_new.astype(jnp.bfloat16)
        acc_ref[0:1, :] += by_lane(weights * weights)
        acc_ref[1:2, :] += by_lane(update * update)

        @pl.when(step == steps - 1)
        def _():
            sums_ref[...] = jnp.broadcast_to(acc_ref[0:2, :][None], sums_ref.shape)

    block = pl.BlockSpec((rows, f_blk), lambda i: (i, 0))
    return pl.pallas_call(
        kernel,
        grid=(steps,),
        in_specs=[pl.BlockSpec(squares.shape, lambda i: (0, 0, 0))] + [block] * 4,
        out_specs=[block] * 3 + [pl.BlockSpec((peers, 2, 128), lambda i: (0, 0, 0))],
        out_shape=[
            jax.ShapeDtypeStruct((d_blk, f_blk), jnp.float32),
            jax.ShapeDtypeStruct((d_blk, f_blk), jnp.bfloat16),
            jax.ShapeDtypeStruct((d_blk, f_blk), jnp.bfloat16),
            jax.ShapeDtypeStruct((peers, 2, 128), jnp.float32),
        ],
        scratch_shapes=[pltpu.VMEM((8, 128), jnp.float32), pltpu.VMEM((8, 128), jnp.float32)],
        compiler_params=pltpu.CompilerParams(vmem_limit_bytes=VMEM_LIMIT),
        name="update_of",
    )(squares, gradient, master, moment, second)


def weights_of(sums, update, master):
    d_blk, f_blk = update.shape
    steps = 4
    rows = d_blk // steps

    def kernel(sums_ref, u_ref, w_ref, out_ref, upper_ref, lower_ref, rate_ref):
        step = pl.program_id(0)

        @pl.when(step == 0)
        def _():
            weight_sq = across(sums_ref[:, 0, :])
            update_sq = across(sums_ref[:, 1, :])
            trust_ratio = jnp.sqrt(weight_sq) / (jnp.sqrt(update_sq) + 1e-06)
            rate_ref[...] = jnp.broadcast_to(0.08 * trust_ratio, rate_ref.shape)

        new = w_ref[...] - rate_ref[0:1, 0:1] * u_ref[...]
        out_ref[...] = new

        @pl.when(step < steps // 2)
        def _():
            upper_ref[...] = new.astype(jnp.bfloat16)

        @pl.when(step >= steps // 2)
        def _():
            lower_ref[...] = new.astype(jnp.bfloat16)

    block = pl.BlockSpec((rows, f_blk), lambda i: (i, 0))
    half = jax.ShapeDtypeStruct((d_blk // 2, f_blk), jnp.bfloat16)
    return pl.pallas_call(
        kernel,
        grid=(steps,),
        in_specs=[pl.BlockSpec(sums.shape, lambda i: (0, 0, 0)), block, block],
        out_specs=[
            block,
            pl.BlockSpec((rows, f_blk), lambda i: (jnp.minimum(i, steps // 2 - 1), 0)),
            pl.BlockSpec((rows, f_blk), lambda i: (jnp.maximum(i - steps // 2, 0), 0)),
        ],
        out_shape=[jax.ShapeDtypeStruct((d_blk, f_blk), jnp.float32), half, half],
        scratch_shapes=[pltpu.VMEM((8, 128), jnp.float32)],
        compiler_params=pltpu.CompilerParams(vmem_limit_bytes=VMEM_LIMIT),
        name="weights_of",
    )(sums, update, master)


def outer_sum(rows, places, pieces, before=None, last=False):
    size_x, _, cap, d_blk = rows.shape
    f_blk = pieces[0][0].shape[-1]
    flat = [part for piece in pieces for part in piece]
    depth = size_x * cap
    n = len(pieces)

    def kernel(*refs):
        refs = list(refs)
        rows_ref = refs.pop(0)
        flat_refs = [refs.pop(0) for _ in flat]
        before_ref = refs.pop(0) if before is not None else None
        total_ref = refs.pop(0)
        square_ref = refs.pop(0) if last else None
        left, right, sems = refs
        q = lax.rem(lax.axis_index("z"), 2)
        copies = []
        at = 0
        for i, piece in enumerate(pieces):
            start = 0
            for part in piece:
                size = part.shape[0]
                copies.append((flat_refs[at], right.at[i, pl.ds(start, size)]))
                start += size
                at += 1
            copies.append((rows_ref.at[:, places[i](q)], left.at[i]))
        fetch(copies, sems)
        if before is None:
            total_ref[...] = jnp.zeros_like(total_ref)
        else:
            total_ref[...] = before_ref[...]

        def add(step, carry):
            i, at = step // 2, pl.multiple_of(lax.rem(step, 2) * (d_blk // 2), 128)
            here = pl.ds(at, d_blk // 2)
            total_ref[here, :] += lax.dot_general(
                left[i, :, :, here].reshape(depth, d_blk // 2),
                right[i].reshape(depth, f_blk),
                (((0,), (0,)), ((), ())),
                preferred_element_type=jnp.float32,
            )
            return carry

        lax.fori_loop(0, 2 * n, add, 0)
        if last:
            value = total_ref[...]
            square_ref[...] = jnp.broadcast_to(by_lane(value * value)[None], square_ref.shape)

    operands = [rows, *flat]
    in_specs = [ANYWHERE] * (1 + len(flat))
    operands[0] = pltpu.with_memory_space_constraint(rows, pltpu.HBM)
    aliases = {}
    if before is not None:
        aliases = {len(operands): 0}
        operands.append(before)
        in_specs.append(IN_VMEM)
    out_shape = [jax.ShapeDtypeStruct((d_blk, f_blk), jnp.float32)]
    if last:
        out_shape.append(jax.ShapeDtypeStruct((lax.axis_size(EVERYONE), 1, 128), jnp.float32))
    return pl.pallas_call(
        kernel,
        in_specs=in_specs,
        out_specs=[IN_VMEM] * len(out_shape),
        out_shape=out_shape,
        scratch_shapes=[
            pltpu.VMEM((n, size_x, cap, d_blk), jnp.bfloat16),
            pltpu.VMEM((n, size_x, cap, f_blk), jnp.bfloat16),
            pltpu.SemaphoreType.DMA((len(flat) + n,)),
        ],
        input_output_aliases=aliases,
        cost_estimate=pl.CostEstimate(
            flops=2 * n * depth * d_blk * f_blk,
            bytes_accessed=n * depth * (d_blk + f_blk) * 2 + 4 * d_blk * f_blk,
            transcendentals=0,
        ),
        compiler_params=pltpu.CompilerParams(vmem_limit_bytes=VMEM_LIMIT),
        name="outer_last" if last else "outer_first" if before is None else "outer_next",
    )(*operands)


def project(tokens, tiles, before=None, last=False):
    size_x, cap, d = tokens.shape
    d_blk = d // GRID_R
    f_blk = tiles[0][1][0].shape[-1]
    flat = [part for _, piece in tiles for part in piece]
    evens = [i for i, (away, _) in enumerate(tiles) if away % 2 == 0]
    odds = [i for i, (away, _) in enumerate(tiles) if away % 2]
    assert evens + odds == list(range(len(tiles)))
    count = size_x * cap
    n = len(tiles)

    def kernel(*refs):
        refs = list(refs)
        tokens_ref = refs.pop(0)
        flat_refs = [refs.pop(0) for _ in flat]
        before_ref = None if before is None else refs.pop(0)
        out_ref, left, right, total, sems = refs
        z = lax.axis_index("z")
        copies = []
        at = 0
        for i, (away, piece) in enumerate(tiles):
            start = 0
            for part in piece:
                size = part.shape[0]
                copies.append((flat_refs[at], right.at[i, pl.ds(start, size)]))
                start += size
                at += 1
            block = lax.rem(z + away + 8, 8) // 2
            columns = pl.ds(pl.multiple_of(block * d_blk, 128), d_blk)
            copies.append((tokens_ref.at[:, :, columns], left.at[i]))
        fetch(copies, sems)

        def add(i, carry):
            total[...] += jnp.dot(
                left[i].reshape(count, d_blk), right[i], preferred_element_type=jnp.float32
            )
            return carry

        for i, steps in enumerate(((0, len(evens)), (len(evens), n))):
            total[...] = jnp.zeros_like(total) if before is None else before_ref[i]
            if steps[0] < steps[1]:
                lax.fori_loop(*steps, add, 0)
            if last:
                out_ref[:, i] = total[...].astype(jnp.bfloat16).reshape(size_x, cap, f_blk)
            else:
                out_ref[i] = total[...]

    if last:
        out_shape = jax.ShapeDtypeStruct((size_x, 2, cap, f_blk), jnp.bfloat16)
    else:
        out_shape = jax.ShapeDtypeStruct((2, count, f_blk), jnp.float32)
    operands = [pltpu.with_memory_space_constraint(tokens, pltpu.HBM), *flat] + ([] if before is None else [before])
    return pl.pallas_call(
        kernel,
        in_specs=[ANYWHERE] * (1 + len(flat)) + [IN_VMEM] * (len(operands) - 1 - len(flat)),
        out_specs=IN_VMEM,
        out_shape=out_shape,
        scratch_shapes=[
            pltpu.VMEM((n, size_x, cap, d_blk), jnp.bfloat16),
            pltpu.VMEM((n, d_blk, f_blk), jnp.bfloat16),
            pltpu.VMEM((count, f_blk), jnp.float32),
            pltpu.SemaphoreType.DMA((len(flat) + n,)),
        ],
        cost_estimate=pl.CostEstimate(
            flops=2 * n * count * d_blk * f_blk,
            bytes_accessed=n * d_blk * (count + f_blk) * 2,
            transcendentals=0,
        ),
        compiler_params=pltpu.CompilerParams(vmem_limit_bytes=VMEM_LIMIT),
        name="project_last" if last else "project_first" if before is None else "project_next",
    )(*operands)


def assemble(found):
    size_x, _, cap, f_blk = found.shape

    def kernel(found_ref, out_ref):
        q = lax.rem(lax.axis_index("z"), 2)
        for i in range(2):
            parity = q if i == 0 else 1 - q
            for j in range(size_x):
                start = pl.multiple_of((parity * size_x + j) * f_blk, 128)
                out_ref[:, pl.ds(start, f_blk)] = found_ref[j, i]

    return pl.pallas_call(
        kernel,
        in_specs=[IN_VMEM],
        out_specs=IN_VMEM,
        out_shape=jax.ShapeDtypeStruct((cap, 2 * size_x * f_blk), found.dtype),
        compiler_params=pltpu.CompilerParams(vmem_limit_bytes=VMEM_LIMIT),
        name="assemble",
    )(found)


def body(activations, out_grads, next_inputs, counts, master, moment, second):
    cap, d = activations.shape[2:]
    ff = out_grads.shape[3]
    d_blk, f_blk = master.shape[2:]
    size_x = lax.axis_size("x")

    own, other, row0, row_p1, row_m1, row_2 = split(
        counts, activations[0, 0], out_grads[0, 0], d_blk, f_blk
    )

    rows = [row0, shift(row_p1, "z", 2), shift(row_m1, "z", -2), shift(row_2, "z", 4)]
    other = exchanged(other, "x")
    other, rows = lax.optimization_barrier((other, jnp.stack(rows)))
    beside = lax.ppermute(rows, "z", [(i, i ^ 1) for i in range(lax.axis_size("z"))])
    place_of = {
        0: lambda q: 0,
        -2: lambda q: 1,
        2: lambda q: 2,
        4: lambda q: 3,
        1: lambda q: 4 + 2 * q,
        -1: lambda q: 5 - q,
        3: lambda q: 6 + q,
        -3: lambda q: 7 - 2 * q,
    }

    other_m1, other_p1 = shift(other, "z", 1), shift(other, "z", -1)
    own, beside, other_m1, other_p1 = lax.optimization_barrier((own, beside, other_m1, other_p1))
    rows = lax.all_gather(jnp.concatenate([rows, beside]), "x")
    own = exchanged(own, "x")
    other_m3, other_p3 = shift(other_m1, "z", 2), shift(other_p1, "z", -2)
    own, other_m3, other_p3 = lax.optimization_barrier((own, other_m3, other_p3))
    own_m2, own_p2 = shift(own, "z", 2), shift(own, "z", -2)
    pieces = {0: [own], -1: [other_m1], 1: [other_p1], -3: [other_m3], 3: [other_p3]}
    pieces |= {-2: [own_m2], 2: [own_p2]}
    first_away = (0, -1, 1, -3, 3)
    next_away = (-2, 2)
    last_away = (4,)
    (gradient,) = outer_sum(
        rows, [place_of[a] for a in first_away], [pieces[a] for a in first_away]
    )
    half = size_x // 2
    up, down = own_m2[:half], own_p2[half:]
    pieces[4] = [shift(up, "z", 2), shift(down, "z", -2)]
    late_inputs, gradient = lax.optimization_barrier((next_inputs[0, 0], gradient))
    tokens = lax.all_gather(late_inputs, "x")
    (gradient,) = outer_sum(
        rows,
        [place_of[a] for a in next_away],
        [pieces[a] for a in next_away],
        before=gradient,
    )
    gradient, squares = outer_sum(
        rows,
        [place_of[a] for a in last_away],
        [pieces[a] for a in last_away],
        before=gradient,
        last=True,
    )

    entries = float(lax.axis_size(EXPERT) * d * ff)
    update, first_new, later_new, sums = update_of(
        exchanged(squares, EVERYONE), gradient, master[0, 0], moment[0, 0], second[0, 0], entries
    )
    weights_new, upper, lower = weights_of(exchanged(sums, SHARD), update, master[0, 0])

    up = [[upper], [lower]]
    down = [[upper], [lower]]
    for step in range(1, 4):
        for c in range(2):
            up[c].append(shift(up[c][-1], "z", 1))
            down[c].append(shift(down[c][-1], "z", -1))
    tiles = [(0, [upper, lower])]
    for away in (2, 1):
        tiles.append((-away, [up[0][away], up[1][away]]))
        tiles.append((away, [down[0][away], down[1][away]]))
    part = project(tokens, tiles)
    part, last_up, last_down = lax.optimization_barrier((part, up[0][3], down[1][3]))
    last_tile = [shift(last_up, "z", 1), shift(last_down, "z", -1)]
    tiles = [(-3, [up[0][3], up[1][3]]), (3, [down[0][3], down[1][3]])]
    part = project(tokens, tiles, before=part)
    found = project(tokens, [(4, last_tile)], before=part, last=True)
    projected = assemble(exchanged(found, "x"))
    return (
        weights_new[None, None],
        first_new[None, None],
        later_new[None, None],
        projected[None, None],
    )


def solution(mesh):
    finer = Mesh(mesh.devices.reshape(4, 2, 8, 4), EVERYONE)
    tiled = P(EXPERT, SHARD, None, None)
    return jax.shard_map(
        body,
        mesh=finer,
        in_specs=(tiled, tiled, tiled, P(EXPERT, SHARD), tiled, tiled, tiled),
        out_specs=(tiled,) * 4,
        check_vma=False,
    )
```

```python
import functools

import jax
import jax.numpy as jnp
from jax import lax
from jax.experimental import pallas as pl
from jax.experimental.pallas import tpu as pltpu
from jax.sharding import Mesh
from jax.sharding import PartitionSpec as P

GRID_R = 4
GRID_C = 8
EXPERT = ("y", "k")
SHARD = ("r", "q", "x")
EVERYONE = ("y", "k", "r", "q", "x")
Z = ("r", "q")


def shift(value, by):
    size = lax.axis_size(Z)
    return lax.ppermute(value, Z, [(i, (i + by) % size) for i in range(size)])


VMEM_LIMIT = 20 << 20
ANYWHERE = pl.BlockSpec(memory_space=pl.ANY)
IN_VMEM = pl.BlockSpec(memory_space=pltpu.VMEM)
IN_SMEM = pl.BlockSpec(memory_space=pltpu.SMEM)


def split(counts, activations, out_grads, d_blk, f_blk):
    cap = activations.shape[0]
    size_x = out_grads.shape[1] // (2 * f_blk)

    def kernel(count_ref, rows_ref, cols_ref, own_ref, other_ref, *row_refs):
        q = lax.axis_index("q")
        valid = lax.broadcasted_iota(jnp.int32, (cap, f_blk), 0) < count_ref[0, 0]
        for i, by in enumerate((0, 1, 3, 2)):
            start = pl.multiple_of(lax.rem(lax.axis_index("r") + by, GRID_R) * d_blk, 128)
            row_refs[i][...] = rows_ref[:, pl.ds(start, d_blk)]
        for ref, parity in ((own_ref, q), (other_ref, 1 - q)):
            for to_x in range(size_x):
                start = pl.multiple_of((parity * size_x + to_x) * f_blk, 128)
                block = cols_ref[:, pl.ds(start, f_blk)].astype(jnp.float32)
                ref[to_x] = jnp.where(valid, block, 0.0).astype(jnp.bfloat16)

    cols = jax.ShapeDtypeStruct((size_x, cap, f_blk), jnp.bfloat16)
    row = jax.ShapeDtypeStruct((cap, d_blk), jnp.bfloat16)
    return pl.pallas_call(
        kernel,
        in_specs=[IN_SMEM, IN_VMEM, IN_VMEM],
        out_specs=[IN_VMEM] * 6,
        out_shape=[cols] * 2 + [row] * 4,
        compiler_params=pltpu.CompilerParams(vmem_limit_bytes=VMEM_LIMIT),
        name="split",
    )(counts, activations, out_grads)


def fetch(copies, sems):
    started = [pltpu.make_async_copy(src, dst, sems.at[i]) for i, (src, dst) in enumerate(copies)]
    for copy in started:
        copy.start()
    for copy in started:
        copy.wait()


def by_lane(values):
    values = jnp.sum(values, axis=0, keepdims=True)
    return sum(values[:, i : i + 128] for i in range(0, values.shape[1], 128))


def across(values):
    return jnp.sum(jnp.sum(values, axis=0, keepdims=True), axis=1, keepdims=True)


def exchanged(values, axes):
    return lax.all_to_all(values, axes, 0, 0, tiled=True)


def update_of(squares, gradient, master, moment, second, entries):
    d_blk, f_blk = gradient.shape
    steps = 4
    rows = d_blk // steps
    peers = lax.axis_size(SHARD)

    def kernel(n_ref, g_ref, w_ref, m_ref, v_ref, u_ref, m_out, v_out, sums_ref, clip_ref, acc_ref):
        step = pl.program_id(0)

        @pl.when(step == 0)
        def _():
            grad_rms = jnp.sqrt(across(n_ref[:, 0, :]) / entries + 1e-06)
            clip_ref[...] = jnp.broadcast_to(jnp.minimum(1.0, 1.0 / grad_rms), clip_ref.shape)
            acc_ref[...] = jnp.zeros_like(acc_ref)

        weights = w_ref[...]
        clipped = clip_ref[0:1, 0:1] * g_ref[...]
        first_new = 0.9 * m_ref[...].astype(jnp.float32) + 0.1 * clipped
        later_new = 0.999 * v_ref[...].astype(jnp.float32) + 0.001 * clipped * clipped
        update = (
            first_new / (1.0 - 0.9**10) / (jnp.sqrt(later_new / (1.0 - 0.999**10)) + 1e-06)
            + 0.01 * weights
        )
        u_ref[...] = update
        m_out[...] = first_new.astype(jnp.bfloat16)
        v_out[...] = later_new.astype(jnp.bfloat16)
        acc_ref[0:1, :] += by_lane(weights * weights)
        acc_ref[1:2, :] += by_lane(update * update)

        @pl.when(step == steps - 1)
        def _():
            sums_ref[...] = jnp.broadcast_to(acc_ref[0:2, :][None], sums_ref.shape)

    block = pl.BlockSpec((rows, f_blk), lambda i: (i, 0))
    return pl.pallas_call(
        kernel,
        grid=(steps,),
        in_specs=[pl.BlockSpec(squares.shape, lambda i: (0, 0, 0))] + [block] * 4,
        out_specs=[block] * 3 + [pl.BlockSpec((peers, 2, 128), lambda i: (0, 0, 0))],
        out_shape=[
            jax.ShapeDtypeStruct((d_blk, f_blk), jnp.float32),
            jax.ShapeDtypeStruct((d_blk, f_blk), jnp.bfloat16),
            jax.ShapeDtypeStruct((d_blk, f_blk), jnp.bfloat16),
            jax.ShapeDtypeStruct((peers, 2, 128), jnp.float32),
        ],
        scratch_shapes=[pltpu.VMEM((8, 128), jnp.float32), pltpu.VMEM((8, 128), jnp.float32)],
        compiler_params=pltpu.CompilerParams(vmem_limit_bytes=VMEM_LIMIT),
        name="update_of",
    )(squares, gradient, master, moment, second)


def weights_of(sums, update, master):
    d_blk, f_blk = update.shape
    steps = 4
    rows = d_blk // steps

    def kernel(sums_ref, u_ref, w_ref, out_ref, upper_ref, lower_ref, rate_ref):
        step = pl.program_id(0)

        @pl.when(step == 0)
        def _():
            weight_sq = across(sums_ref[:, 0, :])
            update_sq = across(sums_ref[:, 1, :])
            trust_ratio = jnp.sqrt(weight_sq) / (jnp.sqrt(update_sq) + 1e-06)
            rate_ref[...] = jnp.broadcast_to(0.08 * trust_ratio, rate_ref.shape)

        new = w_ref[...] - rate_ref[0:1, 0:1] * u_ref[...]
        out_ref[...] = new

        @pl.when(step < steps // 2)
        def _():
            upper_ref[...] = new.astype(jnp.bfloat16)

        @pl.when(step >= steps // 2)
        def _():
            lower_ref[...] = new.astype(jnp.bfloat16)

    block = pl.BlockSpec((rows, f_blk), lambda i: (i, 0))
    half = jax.ShapeDtypeStruct((d_blk // 2, f_blk), jnp.bfloat16)
    return pl.pallas_call(
        kernel,
        grid=(steps,),
        in_specs=[pl.BlockSpec(sums.shape, lambda i: (0, 0, 0)), block, block],
        out_specs=[
            block,
            pl.BlockSpec((rows, f_blk), lambda i: (jnp.minimum(i, steps // 2 - 1), 0)),
            pl.BlockSpec((rows, f_blk), lambda i: (jnp.maximum(i - steps // 2, 0), 0)),
        ],
        out_shape=[jax.ShapeDtypeStruct((d_blk, f_blk), jnp.float32), half, half],
        scratch_shapes=[pltpu.VMEM((8, 128), jnp.float32)],
        compiler_params=pltpu.CompilerParams(vmem_limit_bytes=VMEM_LIMIT),
        name="weights_of",
    )(sums, update, master)


def outer_sum(rows, places, pieces, before=None, last=False):
    size_x, _, cap, d_blk = rows.shape
    f_blk = pieces[0][0].shape[-1]
    flat = [part for piece in pieces for part in piece]
    depth = size_x * cap
    n = len(pieces)

    def kernel(*refs):
        refs = list(refs)
        rows_ref = refs.pop(0)
        flat_refs = [refs.pop(0) for _ in flat]
        before_ref = refs.pop(0) if before is not None else None
        total_ref = refs.pop(0)
        square_ref = refs.pop(0) if last else None
        left, right, sems = refs
        q = lax.axis_index("q")
        copies = []
        at = 0
        for i, piece in enumerate(pieces):
            start = 0
            for part in piece:
                size = part.shape[0]
                copies.append((flat_refs[at], right.at[i, pl.ds(start, size)]))
                start += size
                at += 1
            copies.append((rows_ref.at[:, places[i](q)], left.at[i]))
        fetch(copies, sems)
        if before is None:
            total_ref[...] = jnp.zeros_like(total_ref)
        else:
            total_ref[...] = before_ref[...]

        def add(step, carry):
            i, at = step // 2, pl.multiple_of(lax.rem(step, 2) * (d_blk // 2), 128)
            here = pl.ds(at, d_blk // 2)
            total_ref[here, :] += lax.dot_general(
                left[i, :, :, here].reshape(depth, d_blk // 2),
                right[i].reshape(depth, f_blk),
                (((0,), (0,)), ((), ())),
                preferred_element_type=jnp.float32,
            )
            return carry

        lax.fori_loop(0, 2 * n, add, 0)
        if last:
            value = total_ref[...]
            square_ref[...] = jnp.broadcast_to(by_lane(value * value)[None], square_ref.shape)

    operands = [rows, *flat]
    in_specs = [ANYWHERE] * (1 + len(flat))
    operands[0] = pltpu.with_memory_space_constraint(rows, pltpu.HBM)
    aliases = {}
    if before is not None:
        aliases = {len(operands): 0}
        operands.append(before)
        in_specs.append(IN_VMEM)
    out_shape = [jax.ShapeDtypeStruct((d_blk, f_blk), jnp.float32)]
    if last:
        out_shape.append(jax.ShapeDtypeStruct((lax.axis_size(EVERYONE), 1, 128), jnp.float32))
    return pl.pallas_call(
        kernel,
        in_specs=in_specs,
        out_specs=[IN_VMEM] * len(out_shape),
        out_shape=out_shape,
        scratch_shapes=[
            pltpu.VMEM((n, size_x, cap, d_blk), jnp.bfloat16),
            pltpu.VMEM((n, size_x, cap, f_blk), jnp.bfloat16),
            pltpu.SemaphoreType.DMA((len(flat) + n,)),
        ],
        input_output_aliases=aliases,
        cost_estimate=pl.CostEstimate(
            flops=2 * n * depth * d_blk * f_blk,
            bytes_accessed=n * depth * (d_blk + f_blk) * 2 + 4 * d_blk * f_blk,
            transcendentals=0,
        ),
        compiler_params=pltpu.CompilerParams(vmem_limit_bytes=VMEM_LIMIT),
        name="outer_last" if last else "outer_first" if before is None else "outer_next",
    )(*operands)


def project(tokens, tiles, before=None, last=False):
    shards, cap, d = tokens.shape
    d_blk = d // GRID_R
    f_blk = tiles[0][1][0].shape[-1]
    flat = [part for _, piece in tiles for part in piece]
    count = shards * cap
    n = len(tiles)

    def kernel(*refs):
        refs = list(refs)
        tokens_ref = refs.pop(0)
        flat_refs = [refs.pop(0) for _ in flat]
        before_ref = None if before is None else refs.pop(0)
        out_ref, left, right, total, sems = refs
        copies = []
        at = 0
        for i, (away, piece) in enumerate(tiles):
            start = 0
            for part in piece:
                size = part.shape[0]
                copies.append((flat_refs[at], right.at[i, pl.ds(start, size)]))
                start += size
                at += 1
            block = lax.rem(lax.axis_index("r") + away, GRID_R)
            columns = pl.ds(pl.multiple_of(block * d_blk, 128), d_blk)
            copies.append((tokens_ref.at[:, :, columns], left.at[i]))
        fetch(copies, sems)
        total[...] = jnp.zeros_like(total) if before is None else before_ref[...]
        half = shards // 2

        def add(step, carry):
            i, here = step // 2, lax.rem(step, 2)
            rows = pl.ds(pl.multiple_of(here * half * cap, 8), half * cap)
            total[rows, :] += jnp.dot(
                left[i, pl.ds(here * half, half)].reshape(half * cap, d_blk),
                right[i],
                preferred_element_type=jnp.float32,
            )
            return carry

        lax.fori_loop(0, 2 * n, add, 0)
        if last:
            out_ref[...] = total[...].astype(jnp.bfloat16).reshape(shards, cap, f_blk)
        else:
            out_ref[...] = total[...]

    if last:
        out_shape = jax.ShapeDtypeStruct((shards, cap, f_blk), jnp.bfloat16)
    else:
        out_shape = jax.ShapeDtypeStruct((count, f_blk), jnp.float32)
    operands = [pltpu.with_memory_space_constraint(tokens, pltpu.HBM), *flat]
    operands += [] if before is None else [before]
    return pl.pallas_call(
        kernel,
        in_specs=[ANYWHERE] * (1 + len(flat)) + [IN_VMEM] * (len(operands) - 1 - len(flat)),
        out_specs=IN_VMEM,
        out_shape=out_shape,
        scratch_shapes=[
            pltpu.VMEM((n, shards, cap, d_blk), jnp.bfloat16),
            pltpu.VMEM((n, d_blk, f_blk), jnp.bfloat16),
            pltpu.VMEM((count, f_blk), jnp.float32),
            pltpu.SemaphoreType.DMA((len(flat) + n,)),
        ],
        cost_estimate=pl.CostEstimate(
            flops=2 * n * count * d_blk * f_blk,
            bytes_accessed=n * d_blk * (count + f_blk) * 2,
            transcendentals=0,
        ),
        compiler_params=pltpu.CompilerParams(vmem_limit_bytes=VMEM_LIMIT),
        name="project_last" if last else "project_first" if before is None else "project_next",
    )(*operands)


def assemble(found):
    blocks, cap, f_blk = found.shape

    def kernel(found_ref, out_ref):
        for i in range(blocks):
            out_ref[:, i * f_blk : (i + 1) * f_blk] = found_ref[i]

    return pl.pallas_call(
        kernel,
        in_specs=[IN_VMEM],
        out_specs=IN_VMEM,
        out_shape=jax.ShapeDtypeStruct((cap, blocks * f_blk), found.dtype),
        compiler_params=pltpu.CompilerParams(vmem_limit_bytes=VMEM_LIMIT),
        name="assemble",
    )(found)


def body(activations, out_grads, next_inputs, counts, master, moment, second):
    cap, d = activations.shape[2:]
    ff = out_grads.shape[3]
    d_blk, f_blk = master.shape[2:]
    size_x = lax.axis_size("x")

    own, other, row0, row_p1, row_m1, row_2 = split(
        counts, activations[0, 0], out_grads[0, 0], d_blk, f_blk
    )

    rows = [row0, shift(row_p1, 2), shift(row_m1, -2), shift(row_2, 4)]
    other = exchanged(other, "x")
    other, rows = lax.optimization_barrier((other, jnp.stack(rows)))
    beside = lax.ppermute(rows, "q", [(0, 1), (1, 0)])
    place_of = {
        0: lambda q: 0,
        -2: lambda q: 1,
        2: lambda q: 2,
        4: lambda q: 3,
        1: lambda q: 4 + 2 * q,
        -1: lambda q: 5 - q,
        3: lambda q: 6 + q,
        -3: lambda q: 7 - 2 * q,
    }

    other_m1, other_p1 = shift(other, 1), shift(other, -1)
    own, beside, other_m1, other_p1 = lax.optimization_barrier((own, beside, other_m1, other_p1))
    rows = lax.all_gather(jnp.concatenate([rows, beside]), "x")
    own = exchanged(own, "x")
    other_m3, other_p3 = shift(other_m1, 2), shift(other_p1, -2)
    own, other_m3, other_p3 = lax.optimization_barrier((own, other_m3, other_p3))
    own_m2, own_p2 = shift(own, 2), shift(own, -2)
    late_inputs, own_m2, own_p2 = lax.optimization_barrier((next_inputs[0, 0], own_m2, own_p2))
    tokens = lax.all_gather(late_inputs, ("q", "x"))
    pieces = {0: [own], -1: [other_m1], 1: [other_p1], -3: [other_m3], 3: [other_p3]}
    pieces |= {-2: [own_m2], 2: [own_p2]}
    first_away = (0, -1, 1, -3, 3)
    next_away = (-2, 2)
    last_away = (4,)
    (gradient,) = outer_sum(
        rows, [place_of[a] for a in first_away], [pieces[a] for a in first_away]
    )
    half = size_x // 2
    up, down = own_m2[:half], own_p2[half:]
    pieces[4] = [shift(up, 2), shift(down, -2)]
    (gradient,) = outer_sum(
        rows,
        [place_of[a] for a in next_away],
        [pieces[a] for a in next_away],
        before=gradient,
    )
    gradient, squares = outer_sum(
        rows,
        [place_of[a] for a in last_away],
        [pieces[a] for a in last_away],
        before=gradient,
        last=True,
    )

    entries = float(lax.axis_size(EXPERT) * d * ff)
    update, first_new, later_new, sums = update_of(
        exchanged(squares, EVERYONE), gradient, master[0, 0], moment[0, 0], second[0, 0], entries
    )
    weights_new, upper, lower = weights_of(exchanged(sums, SHARD), update, master[0, 0])

    upper_m, upper_p = shift(upper, 2), shift(upper, -2)
    lower_m, lower_p = shift(lower, 2), shift(lower, -2)
    opposite = [shift(upper_m, 2), shift(lower_p, -2)]
    part = project(tokens, [(0, [upper, lower])])
    part = project(tokens, [(3, [upper_m, lower_m]), (1, [upper_p, lower_p])], before=part)
    found = project(tokens, [(2, opposite)], before=part, last=True)
    projected = assemble(exchanged(found, ("q", "x")))
    return (
        weights_new[None, None],
        first_new[None, None],
        later_new[None, None],
        projected[None, None],
    )


def solution(mesh):
    finer = Mesh(mesh.devices.reshape(4, 2, 4, 2, 4), EVERYONE)
    tiled = P(EXPERT, SHARD, None, None)
    return jax.shard_map(
        body,
        mesh=finer,
        in_specs=(tiled, tiled, tiled, P(EXPERT, SHARD), tiled, tiled, tiled),
        out_specs=(tiled,) * 4,
        check_vma=False,
    )
```

```python
import functools

import jax
import jax.numpy as jnp
from jax import lax
from jax.experimental import pallas as pl
from jax.experimental.pallas import tpu as pltpu
from jax.sharding import Mesh
from jax.sharding import PartitionSpec as P

GRID_R = 4
GRID_C = 8
EXPERT = ("y", "k")
SHARD = ("r", "q", "x")
EVERYONE = ("y", "k", "r", "q", "x")
Z = ("r", "q")


def shift(value, by):
    size = lax.axis_size(Z)
    return lax.ppermute(value, Z, [(i, (i + by) % size) for i in range(size)])


VMEM_LIMIT = 20 << 20
ANYWHERE = pl.BlockSpec(memory_space=pl.ANY)
IN_VMEM = pl.BlockSpec(memory_space=pltpu.VMEM)
IN_SMEM = pl.BlockSpec(memory_space=pltpu.SMEM)


def split(counts, activations, out_grads, d_blk, f_blk):
    cap = activations.shape[0]
    size_x = out_grads.shape[1] // (2 * f_blk)

    def kernel(count_ref, rows_ref, cols_ref, own_ref, other_ref, *row_refs):
        q = lax.axis_index("q")
        valid = lax.broadcasted_iota(jnp.int32, (cap, f_blk), 0) < count_ref[0, 0]
        for i, by in enumerate((0, 1, 3, 2)):
            start = pl.multiple_of(lax.rem(lax.axis_index("r") + by, GRID_R) * d_blk, 128)
            row_refs[i][...] = rows_ref[:, pl.ds(start, d_blk)]
        for ref, parity in ((own_ref, q), (other_ref, 1 - q)):
            for to_x in range(size_x):
                start = pl.multiple_of((parity * size_x + to_x) * f_blk, 128)
                block = cols_ref[:, pl.ds(start, f_blk)].astype(jnp.float32)
                ref[to_x] = jnp.where(valid, block, 0.0).astype(jnp.bfloat16)

    cols = jax.ShapeDtypeStruct((size_x, cap, f_blk), jnp.bfloat16)
    row = jax.ShapeDtypeStruct((cap, d_blk), jnp.bfloat16)
    return pl.pallas_call(
        kernel,
        in_specs=[IN_SMEM, IN_VMEM, IN_VMEM],
        out_specs=[IN_VMEM] * 6,
        out_shape=[cols] * 2 + [row] * 4,
        compiler_params=pltpu.CompilerParams(vmem_limit_bytes=VMEM_LIMIT),
        name="split",
    )(counts, activations, out_grads)


def fetch(copies, sems):
    started = [pltpu.make_async_copy(src, dst, sems.at[i]) for i, (src, dst) in enumerate(copies)]
    for copy in started:
        copy.start()
    for copy in started:
        copy.wait()


def by_lane(values):
    values = jnp.sum(values, axis=0, keepdims=True)
    return sum(values[:, i : i + 128] for i in range(0, values.shape[1], 128))


def across(values):
    return jnp.sum(jnp.sum(values, axis=0, keepdims=True), axis=1, keepdims=True)


def exchanged(values, axes):
    return lax.all_to_all(values, axes, 0, 0, tiled=True)


def update_of(squares, gradient, master, moment, second, entries):
    d_blk, f_blk = gradient.shape
    steps = 4
    rows = d_blk // steps
    peers = lax.axis_size(SHARD)

    def kernel(n_ref, g_ref, w_ref, m_ref, v_ref, u_ref, m_out, v_out, sums_ref, clip_ref, acc_ref):
        step = pl.program_id(0)

        @pl.when(step == 0)
        def _():
            grad_rms = jnp.sqrt(across(n_ref[:, 0, :]) / entries + 1e-06)
            clip_ref[...] = jnp.broadcast_to(jnp.minimum(1.0, 1.0 / grad_rms), clip_ref.shape)
            acc_ref[...] = jnp.zeros_like(acc_ref)

        weights = w_ref[...]
        clipped = clip_ref[0:1, 0:1] * g_ref[...]
        first_new = 0.9 * m_ref[...].astype(jnp.float32) + 0.1 * clipped
        later_new = 0.999 * v_ref[...].astype(jnp.float32) + 0.001 * clipped * clipped
        update = (
            first_new / (1.0 - 0.9**10) / (jnp.sqrt(later_new / (1.0 - 0.999**10)) + 1e-06)
            + 0.01 * weights
        )
        u_ref[...] = update
        m_out[...] = first_new.astype(jnp.bfloat16)
        v_out[...] = later_new.astype(jnp.bfloat16)
        acc_ref[0:1, :] += by_lane(weights * weights)
        acc_ref[1:2, :] += by_lane(update * update)

        @pl.when(step == steps - 1)
        def _():
            sums_ref[...] = jnp.broadcast_to(acc_ref[0:2, :][None], sums_ref.shape)

    block = pl.BlockSpec((rows, f_blk), lambda i: (i, 0))
    return pl.pallas_call(
        kernel,
        grid=(steps,),
        in_specs=[pl.BlockSpec(squares.shape, lambda i: (0, 0, 0))] + [block] * 4,
        out_specs=[block] * 3 + [pl.BlockSpec((peers, 2, 128), lambda i: (0, 0, 0))],
        out_shape=[
            jax.ShapeDtypeStruct((d_blk, f_blk), jnp.float32),
            jax.ShapeDtypeStruct((d_blk, f_blk), jnp.bfloat16),
            jax.ShapeDtypeStruct((d_blk, f_blk), jnp.bfloat16),
            jax.ShapeDtypeStruct((peers, 2, 128), jnp.float32),
        ],
        scratch_shapes=[pltpu.VMEM((8, 128), jnp.float32), pltpu.VMEM((8, 128), jnp.float32)],
        compiler_params=pltpu.CompilerParams(vmem_limit_bytes=VMEM_LIMIT),
        name="update_of",
    )(squares, gradient, master, moment, second)


def weights_of(sums, update, master):
    d_blk, f_blk = update.shape
    steps = 4
    rows = d_blk // steps

    def kernel(sums_ref, u_ref, w_ref, out_ref, upper_ref, lower_ref, rate_ref):
        step = pl.program_id(0)

        @pl.when(step == 0)
        def _():
            weight_sq = across(sums_ref[:, 0, :])
            update_sq = across(sums_ref[:, 1, :])
            trust_ratio = jnp.sqrt(weight_sq) / (jnp.sqrt(update_sq) + 1e-06)
            rate_ref[...] = jnp.broadcast_to(0.08 * trust_ratio, rate_ref.shape)

        new = w_ref[...] - rate_ref[0:1, 0:1] * u_ref[...]
        out_ref[...] = new

        @pl.when(step < steps // 2)
        def _():
            upper_ref[...] = new.astype(jnp.bfloat16)

        @pl.when(step >= steps // 2)
        def _():
            lower_ref[...] = new.astype(jnp.bfloat16)

    block = pl.BlockSpec((rows, f_blk), lambda i: (i, 0))
    half = jax.ShapeDtypeStruct((d_blk // 2, f_blk), jnp.bfloat16)
    return pl.pallas_call(
        kernel,
        grid=(steps,),
        in_specs=[pl.BlockSpec(sums.shape, lambda i: (0, 0, 0)), block, block],
        out_specs=[
            block,
            pl.BlockSpec((rows, f_blk), lambda i: (jnp.minimum(i, steps // 2 - 1), 0)),
            pl.BlockSpec((rows, f_blk), lambda i: (jnp.maximum(i - steps // 2, 0), 0)),
        ],
        out_shape=[jax.ShapeDtypeStruct((d_blk, f_blk), jnp.float32), half, half],
        scratch_shapes=[pltpu.VMEM((8, 128), jnp.float32)],
        compiler_params=pltpu.CompilerParams(vmem_limit_bytes=VMEM_LIMIT),
        name="weights_of",
    )(sums, update, master)


def outer_sum(rows, places, pieces, before=None, last=False):
    size_x, _, cap, d_blk = rows.shape
    f_blk = pieces[0][0].shape[-1]
    flat = [part for piece in pieces for part in piece]
    depth = size_x * cap
    n = len(pieces)

    def kernel(*refs):
        refs = list(refs)
        rows_ref = refs.pop(0)
        flat_refs = [refs.pop(0) for _ in flat]
        before_ref = refs.pop(0) if before is not None else None
        total_ref = refs.pop(0)
        square_ref = refs.pop(0) if last else None
        left, right, sems = refs
        q = lax.axis_index("q")
        copies = []
        at = 0
        for i, piece in enumerate(pieces):
            start = 0
            for part in piece:
                size = part.shape[0]
                copies.append((flat_refs[at], right.at[i, pl.ds(start, size)]))
                start += size
                at += 1
            copies.append((rows_ref.at[:, places[i](q)], left.at[i]))
        fetch(copies, sems)
        if before is None:
            total_ref[...] = jnp.zeros_like(total_ref)
        else:
            total_ref[...] = before_ref[...]

        def add(step, carry):
            i, at = step // 2, pl.multiple_of(lax.rem(step, 2) * (d_blk // 2), 128)
            here = pl.ds(at, d_blk // 2)
            total_ref[here, :] += lax.dot_general(
                left[i, :, :, here].reshape(depth, d_blk // 2),
                right[i].reshape(depth, f_blk),
                (((0,), (0,)), ((), ())),
                preferred_element_type=jnp.float32,
            )
            return carry

        lax.fori_loop(0, 2 * n, add, 0)
        if last:
            value = total_ref[...]
            square_ref[...] = jnp.broadcast_to(by_lane(value * value)[None], square_ref.shape)

    operands = [rows, *flat]
    in_specs = [ANYWHERE] * (1 + len(flat))
    operands[0] = pltpu.with_memory_space_constraint(rows, pltpu.HBM)
    aliases = {}
    if before is not None:
        aliases = {len(operands): 0}
        operands.append(before)
        in_specs.append(IN_VMEM)
    out_shape = [jax.ShapeDtypeStruct((d_blk, f_blk), jnp.float32)]
    if last:
        out_shape.append(jax.ShapeDtypeStruct((lax.axis_size(EVERYONE), 1, 128), jnp.float32))
    return pl.pallas_call(
        kernel,
        in_specs=in_specs,
        out_specs=[IN_VMEM] * len(out_shape),
        out_shape=out_shape,
        scratch_shapes=[
            pltpu.VMEM((n, size_x, cap, d_blk), jnp.bfloat16),
            pltpu.VMEM((n, size_x, cap, f_blk), jnp.bfloat16),
            pltpu.SemaphoreType.DMA((len(flat) + n,)),
        ],
        input_output_aliases=aliases,
        cost_estimate=pl.CostEstimate(
            flops=2 * n * depth * d_blk * f_blk,
            bytes_accessed=n * depth * (d_blk + f_blk) * 2 + 4 * d_blk * f_blk,
            transcendentals=0,
        ),
        compiler_params=pltpu.CompilerParams(vmem_limit_bytes=VMEM_LIMIT),
        name="outer_last" if last else "outer_first" if before is None else "outer_next",
    )(*operands)


def project(tokens, tiles, before=None, last=False):
    shards, cap, d = tokens.shape
    d_blk = d // GRID_R
    f_blk = tiles[0][1][0].shape[-1]
    flat = [part for _, piece in tiles for part in piece]
    count = shards * cap
    n = len(tiles)

    def kernel(*refs):
        refs = list(refs)
        tokens_ref = refs.pop(0)
        flat_refs = [refs.pop(0) for _ in flat]
        before_ref = None if before is None else refs.pop(0)
        out_ref, left, right, total, sems = refs
        copies = []
        at = 0
        for i, (away, piece) in enumerate(tiles):
            start = 0
            for part in piece:
                size = part.shape[0]
                copies.append((flat_refs[at], right.at[i, pl.ds(start, size)]))
                start += size
                at += 1
            block = lax.rem(lax.axis_index("r") + away, GRID_R)
            columns = pl.ds(pl.multiple_of(block * d_blk, 128), d_blk)
            copies.append((tokens_ref.at[:, :, columns], left.at[i]))
        fetch(copies, sems)
        total[...] = jnp.zeros_like(total) if before is None else before_ref[...]
        half = shards // 2

        def add(step, carry):
            i, here = step // 2, lax.rem(step, 2)
            rows = pl.ds(pl.multiple_of(here * half * cap, 8), half * cap)
            total[rows, :] += jnp.dot(
                left[i, pl.ds(here * half, half)].reshape(half * cap, d_blk),
                right[i],
                preferred_element_type=jnp.float32,
            )
            return carry

        lax.fori_loop(0, 2 * n, add, 0)
        if last:
            out_ref[...] = total[...].astype(jnp.bfloat16).reshape(shards, cap, f_blk)
        else:
            out_ref[...] = total[...]

    if last:
        out_shape = jax.ShapeDtypeStruct((shards, cap, f_blk), jnp.bfloat16)
    else:
        out_shape = jax.ShapeDtypeStruct((count, f_blk), jnp.float32)
    operands = [pltpu.with_memory_space_constraint(tokens, pltpu.HBM), *flat]
    operands += [] if before is None else [before]
    return pl.pallas_call(
        kernel,
        in_specs=[ANYWHERE] * (1 + len(flat)) + [IN_VMEM] * (len(operands) - 1 - len(flat)),
        out_specs=IN_VMEM,
        out_shape=out_shape,
        scratch_shapes=[
            pltpu.VMEM((n, shards, cap, d_blk), jnp.bfloat16),
            pltpu.VMEM((n, d_blk, f_blk), jnp.bfloat16),
            pltpu.VMEM((count, f_blk), jnp.float32),
            pltpu.SemaphoreType.DMA((len(flat) + n,)),
        ],
        cost_estimate=pl.CostEstimate(
            flops=2 * n * count * d_blk * f_blk,
            bytes_accessed=n * d_blk * (count + f_blk) * 2,
            transcendentals=0,
        ),
        compiler_params=pltpu.CompilerParams(vmem_limit_bytes=VMEM_LIMIT),
        name="project_last" if last else "project_first" if before is None else "project_next",
    )(*operands)


def assemble(found):
    blocks, cap, f_blk = found.shape

    def kernel(found_ref, out_ref):
        for i in range(blocks):
            start = (i % 2 * (blocks // 2) + i // 2) * f_blk
            out_ref[:, start : start + f_blk] = found_ref[i]

    return pl.pallas_call(
        kernel,
        in_specs=[IN_VMEM],
        out_specs=IN_VMEM,
        out_shape=jax.ShapeDtypeStruct((cap, blocks * f_blk), found.dtype),
        compiler_params=pltpu.CompilerParams(vmem_limit_bytes=VMEM_LIMIT),
        name="assemble",
    )(found)


def body(activations, out_grads, next_inputs, counts, master, moment, second):
    cap, d = activations.shape[2:]
    ff = out_grads.shape[3]
    d_blk, f_blk = master.shape[2:]
    size_x = lax.axis_size("x")

    own, other, row0, row_p1, row_m1, row_2 = split(
        counts, activations[0, 0], out_grads[0, 0], d_blk, f_blk
    )

    rows = [row0, shift(row_p1, 2), shift(row_m1, -2), shift(row_2, 4)]
    other = exchanged(other, "x")
    mine = next_inputs[0, 0]
    theirs = lax.ppermute(mine, "q", [(0, 1), (1, 0)])
    other, rows, theirs = lax.optimization_barrier((other, jnp.stack(rows), theirs))
    beside = lax.ppermute(rows, "q", [(0, 1), (1, 0)])
    place_of = {
        0: lambda q: 0,
        -2: lambda q: 1,
        2: lambda q: 2,
        4: lambda q: 3,
        1: lambda q: 4 + 2 * q,
        -1: lambda q: 5 - q,
        3: lambda q: 6 + q,
        -3: lambda q: 7 - 2 * q,
    }

    other_m1, other_p1 = shift(other, 1), shift(other, -1)
    own, beside, other_m1, other_p1 = lax.optimization_barrier((own, beside, other_m1, other_p1))
    rows = lax.all_gather(jnp.concatenate([rows, beside]), "x")
    own = exchanged(own, "x")
    other_m3, other_p3 = shift(other_m1, 2), shift(other_p1, -2)
    first = lax.axis_index("q") == 0
    tokens = jnp.stack([jnp.where(first, mine, theirs), jnp.where(first, theirs, mine)])
    own, other_m3, other_p3, tokens = lax.optimization_barrier((own, other_m3, other_p3, tokens))
    tokens = lax.all_gather(tokens, "x").reshape(2 * size_x, cap, d)
    own_m2, own_p2 = shift(own, 2), shift(own, -2)
    pieces = {0: [own], -1: [other_m1], 1: [other_p1], -3: [other_m3], 3: [other_p3]}
    pieces |= {-2: [own_m2], 2: [own_p2]}
    first_away = (0, -1, 1, -3, 3)
    next_away = (-2, 2)
    last_away = (4,)
    (gradient,) = outer_sum(
        rows, [place_of[a] for a in first_away], [pieces[a] for a in first_away]
    )
    half = size_x // 2
    up, down = own_m2[:half], own_p2[half:]
    pieces[4] = [shift(up, 2), shift(down, -2)]
    (gradient,) = outer_sum(
        rows,
        [place_of[a] for a in next_away],
        [pieces[a] for a in next_away],
        before=gradient,
    )
    gradient, squares = outer_sum(
        rows,
        [place_of[a] for a in last_away],
        [pieces[a] for a in last_away],
        before=gradient,
        last=True,
    )

    entries = float(lax.axis_size(EXPERT) * d * ff)
    update, first_new, later_new, sums = update_of(
        exchanged(squares, EVERYONE), gradient, master[0, 0], moment[0, 0], second[0, 0], entries
    )
    weights_new, upper, lower = weights_of(exchanged(sums, SHARD), update, master[0, 0])

    upper_m, upper_p = shift(upper, 2), shift(upper, -2)
    lower_m, lower_p = shift(lower, 2), shift(lower, -2)
    opposite = [shift(upper_m, 2), shift(lower_p, -2)]
    part = project(tokens, [(0, [upper, lower])])
    part = project(tokens, [(3, [upper_m, lower_m]), (1, [upper_p, lower_p])], before=part)
    found = project(tokens, [(2, opposite)], before=part, last=True)
    projected = assemble(exchanged(found, ("x", "q")))
    return (
        weights_new[None, None],
        first_new[None, None],
        later_new[None, None],
        projected[None, None],
    )


def solution(mesh):
    finer = Mesh(mesh.devices.reshape(4, 2, 4, 2, 4), EVERYONE)
    tiled = P(EXPERT, SHARD, None, None)
    return jax.shard_map(
        body,
        mesh=finer,
        in_specs=(tiled, tiled, tiled, P(EXPERT, SHARD), tiled, tiled, tiled),
        out_specs=(tiled,) * 4,
        check_vma=False,
    )
```

```python
import functools

import jax
import jax.numpy as jnp
from jax import lax
from jax.experimental import pallas as pl
from jax.experimental.pallas import tpu as pltpu
from jax.sharding import Mesh
from jax.sharding import PartitionSpec as P

GRID_R = 4
GRID_C = 8
EXPERT = ("y", "k")
SHARD = ("r", "q", "x")
EVERYONE = ("y", "k", "r", "q", "x")
Z = ("r", "q")


def shift(value, by):
    size = lax.axis_size(Z)
    return lax.ppermute(value, Z, [(i, (i + by) % size) for i in range(size)])


VMEM_LIMIT = 20 << 20
ANYWHERE = pl.BlockSpec(memory_space=pl.ANY)
IN_VMEM = pl.BlockSpec(memory_space=pltpu.VMEM)
IN_SMEM = pl.BlockSpec(memory_space=pltpu.SMEM)


def split(counts, activations, out_grads, d_blk, f_blk):
    cap = activations.shape[0]
    size_x = out_grads.shape[1] // (2 * f_blk)

    def kernel(count_ref, rows_ref, cols_ref, own_ref, other_ref, *row_refs):
        q = lax.axis_index("q")
        valid = lax.broadcasted_iota(jnp.int32, (cap, f_blk), 0) < count_ref[0, 0]
        for i, by in enumerate((0, 1, 3, 2)):
            start = pl.multiple_of(lax.rem(lax.axis_index("r") + by, GRID_R) * d_blk, 128)
            row_refs[i][...] = rows_ref[:, pl.ds(start, d_blk)]
        for ref, parity in ((own_ref, q), (other_ref, 1 - q)):
            for to_x in range(size_x):
                start = pl.multiple_of((parity * size_x + to_x) * f_blk, 128)
                block = cols_ref[:, pl.ds(start, f_blk)].astype(jnp.float32)
                ref[to_x] = jnp.where(valid, block, 0.0).astype(jnp.bfloat16)

    cols = jax.ShapeDtypeStruct((size_x, cap, f_blk), jnp.bfloat16)
    row = jax.ShapeDtypeStruct((cap, d_blk), jnp.bfloat16)
    return pl.pallas_call(
        kernel,
        in_specs=[IN_SMEM, IN_VMEM, IN_VMEM],
        out_specs=[IN_VMEM] * 6,
        out_shape=[cols] * 2 + [row] * 4,
        compiler_params=pltpu.CompilerParams(vmem_limit_bytes=VMEM_LIMIT),
        name="split",
    )(counts, activations, out_grads)


def fetch(copies, sems):
    started = [pltpu.make_async_copy(src, dst, sems.at[i]) for i, (src, dst) in enumerate(copies)]
    for copy in started:
        copy.start()
    for copy in started:
        copy.wait()


def by_lane(values):
    values = jnp.sum(values, axis=0, keepdims=True)
    return sum(values[:, i : i + 128] for i in range(0, values.shape[1], 128))


def across(values):
    return jnp.sum(jnp.sum(values, axis=0, keepdims=True), axis=1, keepdims=True)


def exchanged(values, axes):
    return lax.all_to_all(values, axes, 0, 0, tiled=True)


def update_of(squares, gradient, master, moment, second, entries):
    d_blk, f_blk = gradient.shape
    steps = 4
    rows = d_blk // steps
    peers = lax.axis_size(SHARD)

    def kernel(n_ref, g_ref, w_ref, m_ref, v_ref, u_ref, m_out, v_out, sums_ref, clip_ref, acc_ref):
        step = pl.program_id(0)

        @pl.when(step == 0)
        def _():
            grad_rms = jnp.sqrt(across(n_ref[:, 0, :]) / entries + 1e-06)
            clip_ref[...] = jnp.broadcast_to(jnp.minimum(1.0, 1.0 / grad_rms), clip_ref.shape)
            acc_ref[...] = jnp.zeros_like(acc_ref)

        weights = w_ref[...]
        clipped = clip_ref[0:1, 0:1] * g_ref[...]
        first_new = 0.9 * m_ref[...].astype(jnp.float32) + 0.1 * clipped
        later_new = 0.999 * v_ref[...].astype(jnp.float32) + 0.001 * clipped * clipped
        update = (
            first_new / (1.0 - 0.9**10) / (jnp.sqrt(later_new / (1.0 - 0.999**10)) + 1e-06)
            + 0.01 * weights
        )
        u_ref[...] = update
        m_out[...] = first_new.astype(jnp.bfloat16)
        v_out[...] = later_new.astype(jnp.bfloat16)
        acc_ref[0:1, :] += by_lane(weights * weights)
        acc_ref[1:2, :] += by_lane(update * update)

        @pl.when(step == steps - 1)
        def _():
            sums_ref[...] = jnp.broadcast_to(acc_ref[0:2, :][None], sums_ref.shape)

    block = pl.BlockSpec((rows, f_blk), lambda i: (i, 0))
    return pl.pallas_call(
        kernel,
        grid=(steps,),
        in_specs=[pl.BlockSpec(squares.shape, lambda i: (0, 0, 0))] + [block] * 4,
        out_specs=[block] * 3 + [pl.BlockSpec((peers, 2, 128), lambda i: (0, 0, 0))],
        out_shape=[
            jax.ShapeDtypeStruct((d_blk, f_blk), jnp.float32),
            jax.ShapeDtypeStruct((d_blk, f_blk), jnp.bfloat16),
            jax.ShapeDtypeStruct((d_blk, f_blk), jnp.bfloat16),
            jax.ShapeDtypeStruct((peers, 2, 128), jnp.float32),
        ],
        scratch_shapes=[pltpu.VMEM((8, 128), jnp.float32), pltpu.VMEM((8, 128), jnp.float32)],
        compiler_params=pltpu.CompilerParams(vmem_limit_bytes=VMEM_LIMIT),
        name="update_of",
    )(squares, gradient, master, moment, second)


def weights_of(sums, update, master):
    d_blk, f_blk = update.shape
    steps = 4
    rows = d_blk // steps

    def kernel(sums_ref, u_ref, w_ref, out_ref, upper_ref, lower_ref, rate_ref):
        step = pl.program_id(0)

        @pl.when(step == 0)
        def _():
            weight_sq = across(sums_ref[:, 0, :])
            update_sq = across(sums_ref[:, 1, :])
            trust_ratio = jnp.sqrt(weight_sq) / (jnp.sqrt(update_sq) + 1e-06)
            rate_ref[...] = jnp.broadcast_to(0.08 * trust_ratio, rate_ref.shape)

        new = w_ref[...] - rate_ref[0:1, 0:1] * u_ref[...]
        out_ref[...] = new

        @pl.when(step < steps // 2)
        def _():
            upper_ref[...] = new.astype(jnp.bfloat16)

        @pl.when(step >= steps // 2)
        def _():
            lower_ref[...] = new.astype(jnp.bfloat16)

    block = pl.BlockSpec((rows, f_blk), lambda i: (i, 0))
    half = jax.ShapeDtypeStruct((d_blk // 2, f_blk), jnp.bfloat16)
    return pl.pallas_call(
        kernel,
        grid=(steps,),
        in_specs=[pl.BlockSpec(sums.shape, lambda i: (0, 0, 0)), block, block],
        out_specs=[
            block,
            pl.BlockSpec((rows, f_blk), lambda i: (jnp.minimum(i, steps // 2 - 1), 0)),
            pl.BlockSpec((rows, f_blk), lambda i: (jnp.maximum(i - steps // 2, 0), 0)),
        ],
        out_shape=[jax.ShapeDtypeStruct((d_blk, f_blk), jnp.float32), half, half],
        scratch_shapes=[pltpu.VMEM((8, 128), jnp.float32)],
        compiler_params=pltpu.CompilerParams(vmem_limit_bytes=VMEM_LIMIT),
        name="weights_of",
    )(sums, update, master)


def outer_sum(rows, places, pieces, before=None, last=False):
    size_x, _, cap, d_blk = rows.shape
    f_blk = pieces[0][0].shape[-1]
    flat = [part for piece in pieces for part in piece]
    depth = size_x * cap
    n = len(pieces)

    def kernel(*refs):
        refs = list(refs)
        rows_ref = refs.pop(0)
        flat_refs = [refs.pop(0) for _ in flat]
        before_ref = refs.pop(0) if before is not None else None
        total_ref = refs.pop(0)
        square_ref = refs.pop(0) if last else None
        left, right, sems = refs
        q = lax.axis_index("q")
        copies = []
        at = 0
        for i, piece in enumerate(pieces):
            start = 0
            for part in piece:
                size = part.shape[0]
                copies.append((flat_refs[at], right.at[i, pl.ds(start, size)]))
                start += size
                at += 1
            copies.append((rows_ref.at[:, places[i](q)], left.at[i]))
        fetch(copies, sems)
        if before is None:
            total_ref[...] = jnp.zeros_like(total_ref)
        else:
            total_ref[...] = before_ref[...]

        def add(step, carry):
            i, at = step // 2, pl.multiple_of(lax.rem(step, 2) * (d_blk // 2), 128)
            here = pl.ds(at, d_blk // 2)
            total_ref[here, :] += lax.dot_general(
                left[i, :, :, here].reshape(depth, d_blk // 2),
                right[i].reshape(depth, f_blk),
                (((0,), (0,)), ((), ())),
                preferred_element_type=jnp.float32,
            )
            return carry

        lax.fori_loop(0, 2 * n, add, 0)
        if last:
            value = total_ref[...]
            square_ref[...] = jnp.broadcast_to(by_lane(value * value)[None], square_ref.shape)

    operands = [rows, *flat]
    in_specs = [ANYWHERE] * (1 + len(flat))
    operands[0] = pltpu.with_memory_space_constraint(rows, pltpu.HBM)
    aliases = {}
    if before is not None:
        aliases = {len(operands): 0}
        operands.append(before)
        in_specs.append(IN_VMEM)
    out_shape = [jax.ShapeDtypeStruct((d_blk, f_blk), jnp.float32)]
    if last:
        out_shape.append(jax.ShapeDtypeStruct((lax.axis_size(EVERYONE), 1, 128), jnp.float32))
    return pl.pallas_call(
        kernel,
        in_specs=in_specs,
        out_specs=[IN_VMEM] * len(out_shape),
        out_shape=out_shape,
        scratch_shapes=[
            pltpu.VMEM((n, size_x, cap, d_blk), jnp.bfloat16),
            pltpu.VMEM((n, size_x, cap, f_blk), jnp.bfloat16),
            pltpu.SemaphoreType.DMA((len(flat) + n,)),
        ],
        input_output_aliases=aliases,
        cost_estimate=pl.CostEstimate(
            flops=2 * n * depth * d_blk * f_blk,
            bytes_accessed=n * depth * (d_blk + f_blk) * 2 + 4 * d_blk * f_blk,
            transcendentals=0,
        ),
        compiler_params=pltpu.CompilerParams(vmem_limit_bytes=VMEM_LIMIT),
        name="outer_last" if last else "outer_first" if before is None else "outer_next",
    )(*operands)


def project(tokens, tiles, before=None, last=False):
    size_x, cap, d = tokens[0].shape
    shards = 2 * size_x
    d_blk = d // GRID_R
    f_blk = tiles[0][1][0].shape[-1]
    flat = [part for _, piece in tiles for part in piece]
    count = shards * cap
    n = len(tiles)

    def kernel(*refs):
        refs = list(refs)
        tokens_refs = [refs.pop(0), refs.pop(0)]
        flat_refs = [refs.pop(0) for _ in flat]
        before_ref = None if before is None else refs.pop(0)
        out_ref, left, right, total, sems = refs
        copies = []
        at = 0
        for i, (away, piece) in enumerate(tiles):
            start = 0
            for part in piece:
                size = part.shape[0]
                copies.append((flat_refs[at], right.at[i, pl.ds(start, size)]))
                start += size
                at += 1
            block = lax.rem(lax.axis_index("r") + away, GRID_R)
            columns = pl.ds(pl.multiple_of(block * d_blk, 128), d_blk)
            for q, tokens_ref in zip((lax.axis_index("q"), 1 - lax.axis_index("q")), tokens_refs):
                there = left.at[i, pl.ds(q * size_x, size_x)]
                copies.append((tokens_ref.at[:, :, columns], there))
        fetch(copies, sems)
        total[...] = jnp.zeros_like(total) if before is None else before_ref[...]
        half = shards // 2

        def add(step, carry):
            i, here = step // 2, lax.rem(step, 2)
            rows = pl.ds(pl.multiple_of(here * half * cap, 8), half * cap)
            total[rows, :] += jnp.dot(
                left[i, pl.ds(here * half, half)].reshape(half * cap, d_blk),
                right[i],
                preferred_element_type=jnp.float32,
            )
            return carry

        lax.fori_loop(0, 2 * n, add, 0)
        if last:
            out_ref[...] = total[...].astype(jnp.bfloat16).reshape(shards, cap, f_blk)
        else:
            out_ref[...] = total[...]

    if last:
        out_shape = jax.ShapeDtypeStruct((shards, cap, f_blk), jnp.bfloat16)
    else:
        out_shape = jax.ShapeDtypeStruct((count, f_blk), jnp.float32)
    operands = [pltpu.with_memory_space_constraint(t, pltpu.HBM) for t in tokens] + flat
    operands += [] if before is None else [before]
    return pl.pallas_call(
        kernel,
        in_specs=[ANYWHERE] * (2 + len(flat)) + [IN_VMEM] * (len(operands) - 2 - len(flat)),
        out_specs=IN_VMEM,
        out_shape=out_shape,
        scratch_shapes=[
            pltpu.VMEM((n, shards, cap, d_blk), jnp.bfloat16),
            pltpu.VMEM((n, d_blk, f_blk), jnp.bfloat16),
            pltpu.VMEM((count, f_blk), jnp.float32),
            pltpu.SemaphoreType.DMA((len(flat) + 2 * n,)),
        ],
        cost_estimate=pl.CostEstimate(
            flops=2 * n * count * d_blk * f_blk,
            bytes_accessed=n * d_blk * (count + f_blk) * 2,
            transcendentals=0,
        ),
        compiler_params=pltpu.CompilerParams(vmem_limit_bytes=VMEM_LIMIT),
        name="project_last" if last else "project_first" if before is None else "project_next",
    )(*operands)


def assemble(found):
    blocks, cap, f_blk = found.shape

    def kernel(found_ref, out_ref):
        for i in range(blocks):
            start = i * f_blk
            out_ref[:, start : start + f_blk] = found_ref[i]

    return pl.pallas_call(
        kernel,
        in_specs=[IN_VMEM],
        out_specs=IN_VMEM,
        out_shape=jax.ShapeDtypeStruct((cap, blocks * f_blk), found.dtype),
        compiler_params=pltpu.CompilerParams(vmem_limit_bytes=VMEM_LIMIT),
        name="assemble",
    )(found)


def body(activations, out_grads, next_inputs, counts, master, moment, second):
    cap, d = activations.shape[2:]
    ff = out_grads.shape[3]
    d_blk, f_blk = master.shape[2:]
    size_x = lax.axis_size("x")

    own, other, row0, row_p1, row_m1, row_2 = split(
        counts, activations[0, 0], out_grads[0, 0], d_blk, f_blk
    )

    rows = [row0, shift(row_p1, 2), shift(row_m1, -2), shift(row_2, 4)]
    other = exchanged(other, "x")
    mine = next_inputs[0, 0]
    theirs = lax.ppermute(mine, "q", [(0, 1), (1, 0)])
    other, rows, theirs = lax.optimization_barrier((other, jnp.stack(rows), theirs))
    beside = lax.ppermute(rows, "q", [(0, 1), (1, 0)])
    place_of = {
        0: lambda q: 0,
        -2: lambda q: 1,
        2: lambda q: 2,
        4: lambda q: 3,
        1: lambda q: 4 + 2 * q,
        -1: lambda q: 5 - q,
        3: lambda q: 6 + q,
        -3: lambda q: 7 - 2 * q,
    }

    other_m1, other_p1 = shift(other, 1), shift(other, -1)
    own, beside, other_m1, other_p1 = lax.optimization_barrier((own, beside, other_m1, other_p1))
    rows = lax.all_gather(jnp.concatenate([rows, beside]), "x")
    own = exchanged(own, "x")
    other_m3, other_p3 = shift(other_m1, 2), shift(other_p1, -2)
    own, other_m3, other_p3, theirs = lax.optimization_barrier((own, other_m3, other_p3, theirs))
    theirs = lax.all_gather(theirs, "x")
    own_m2, own_p2 = shift(own, 2), shift(own, -2)
    pieces = {0: [own], -1: [other_m1], 1: [other_p1], -3: [other_m3], 3: [other_p3]}
    pieces |= {-2: [own_m2], 2: [own_p2]}
    first_away = (0, -1, 1, -3, 3)
    next_away = (-2, 2)
    last_away = (4,)
    (gradient,) = outer_sum(
        rows, [place_of[a] for a in first_away], [pieces[a] for a in first_away]
    )
    mine, gradient, own_m2, own_p2 = lax.optimization_barrier((mine, gradient, own_m2, own_p2))
    pieces |= {-2: [own_m2], 2: [own_p2]}
    tokens = (lax.all_gather(mine, "x"), theirs)
    half = size_x // 2
    up, down = own_m2[:half], own_p2[half:]
    pieces[4] = [shift(up, 2), shift(down, -2)]
    (gradient,) = outer_sum(
        rows,
        [place_of[a] for a in next_away],
        [pieces[a] for a in next_away],
        before=gradient,
    )
    gradient, squares = outer_sum(
        rows,
        [place_of[a] for a in last_away],
        [pieces[a] for a in last_away],
        before=gradient,
        last=True,
    )

    entries = float(lax.axis_size(EXPERT) * d * ff)
    update, first_new, later_new, sums = update_of(
        exchanged(squares, EVERYONE), gradient, master[0, 0], moment[0, 0], second[0, 0], entries
    )
    weights_new, upper, lower = weights_of(exchanged(sums, SHARD), update, master[0, 0])

    upper_m, upper_p = shift(upper, 2), shift(upper, -2)
    lower_m, lower_p = shift(lower, 2), shift(lower, -2)
    opposite = [shift(upper_m, 2), shift(lower_p, -2)]
    part = project(tokens, [(0, [upper, lower])])
    part = project(tokens, [(3, [upper_m, lower_m]), (1, [upper_p, lower_p])], before=part)
    found = project(tokens, [(2, opposite)], before=part, last=True)
    projected = assemble(exchanged(found, ("q", "x")))
    return (
        weights_new[None, None],
        first_new[None, None],
        later_new[None, None],
        projected[None, None],
    )


def solution(mesh):
    finer = Mesh(mesh.devices.reshape(4, 2, 4, 2, 4), EVERYONE)
    tiled = P(EXPERT, SHARD, None, None)
    return jax.shard_map(
        body,
        mesh=finer,
        in_specs=(tiled, tiled, tiled, P(EXPERT, SHARD), tiled, tiled, tiled),
        out_specs=(tiled,) * 4,
        check_vma=False,
    )
```
